32 devices in a mesh: expert: 8 (over z, x), fsdp: 4 (over y, core).
Axes of the slice: x: 2, y: 2, z: 4, core: 2. Of those that a mesh axis runs over, the one named last changes fastest.
Arguments:
- tokens: bfloat16 [2048, 7168], P('expert', 'fsdp'), may hold values from -6 to 6
- output_grad: bfloat16 [2048, 7168], P('expert', 'fsdp'), may hold values from -6 to 6
- route_weight: float32 [2048, 8], P('expert'), may hold values from 0.05 to 0.5
- expert_ids: int32 [2048, 8], P('expert'), may hold values from 0 to 255, all different within a row; in each aligned block of 256 rows (0 to 255, 256 to 511, ...) at most 12 rows name the same one
- gate_weight: bfloat16 [8, 7168, 512], P('expert', 'fsdp'), may hold values from -0.0625 to 0.0625
- up_weight: bfloat16 [8, 7168, 512], P('expert', 'fsdp'), may hold values from -0.0625 to 0.0625
- down_weight: bfloat16 [8, 512, 7168], P('expert', None, 'fsdp'), may hold values from -0.1875 to 0.1875
Outputs:
- token_grad: bfloat16 [2048, 7168], P('expert', 'fsdp')
- gate_grad: bfloat16 [8, 7168, 512], P('expert', 'fsdp')
- up_grad: bfloat16 [8, 7168, 512], P('expert', 'fsdp')
- down_grad: bfloat16 [8, 512, 7168], P('expert', None, 'fsdp')
The draws below stay inside these ranges and needn't reach their ends.
Inputs may be any that keep to these rules, and one draw needn't show every extreme that they name: `expert_ids`: in each block of 256 rows (the tokens held by one position along `expert` (one block of 256 consecutive rows)) no expert is named by more than 12 rows, a bound that some block reaches.
All inputs are finite; a program needn't handle non-finite values.
Results may differ from the reference program's by a relative error of at most 0.025.
Values may be sent and summed in bfloat16 or wider, within the bound.
No kernel may reach another device: no remote copies, remote signals or barrier semaphores. Data moves between devices by JAX's collectives and lax.ppermute only.
A program may use at most 64 MiB of HBM per device.

```python
import math
import jax
import jax.numpy as jnp
import numpy as np
from jax import lax

D = 7168
FF = 1024
EXPERTS = 256
TOPK = 8
TOK_DEV = 256
HALF = 512
CAP = 12
GROUP = 4
TOKENS = 2048
N_EXPERT = 8
N_FSDP = 4


def levels(key, dims, split, low, high):
    gain = 1.0
    for dim, shards_of in split:
        heights = jax.random.uniform(jax.random.fold_in(jax.random.fold_in(key, 6), dim), (shards_of,), jnp.float32, low / len(split), high / len(split))
        gain = gain * jnp.repeat(jnp.exp(heights), dims[dim] // shards_of).reshape((-1,) + (1,) * (len(dims) - 1 - dim))
    return gain


def deal_out(own_key, own, number, rows, amount, top, reach, lean):
    ranking = jax.random.permutation(own_key, amount)
    heavy_load, common = shares(amount, rows * top, reach, lean, True), shares(amount, rows * top, reach, lean, False)
    places = jnp.arange(amount)

    def named(tallies, offset_by):
        used = int((tallies > 0).sum())
        fixed = max(1, used // 4)
        passed = fixed + (places - fixed + offset_by * (used - fixed)) % max(1, amount - fixed)
        return jnp.zeros((amount,), jnp.int32).at[ranking[jnp.where(places < fixed, places, passed)]].set(jnp.asarray(tallies, jnp.int32))

    tallies = jnp.where(number % 4 == 0, named(heavy_load, number // 4), named(common, number - number // 4 - 1))
    mixed = jax.random.permutation(jax.random.fold_in(own, 3), amount)
    giver, taker = mixed[0:amount // 2 * 2:2], mixed[1:amount // 2 * 2:2]
    room = jnp.minimum(tallies[giver] - 1, reach - tallies[taker]) // 2
    room = jnp.where((giver == ranking[0]) | (taker == ranking[0]) | (tallies[taker] == 0), 0, jnp.maximum(room, 0))
    passed = jax.random.randint(jax.random.fold_in(own, 4), (amount // 2,), 0, 1 << 20) % (room + 1)
    tallies = tallies.at[giver].add(-passed).at[taker].add(passed)
    items = jnp.searchsorted(jnp.cumsum(tallies), jnp.arange(rows * top), side="right").astype(jnp.int32)
    table = items.reshape(top, rows).T
    table = table[jax.random.permutation(jax.random.fold_in(own, 1), rows)]
    offset_by = jax.random.randint(jax.random.fold_in(own, 2), (rows, 1), 0, top)
    return jnp.take_along_axis(table, (jnp.arange(top)[None, :] + offset_by) % top, axis=1)


def shares(amount, total, most, slope, full):
    portions = [(1 << 20) // math.isqrt(rank ** slope) + 1 for rank in range(1, amount + 1)]
    largest = most if full else min(most, max(-(-total // amount), total * portions[0] // sum(portions)))
    least = 1 if total - largest >= amount - 1 else 0
    holding, surplus = [largest] + [least] * (amount - 1), total - largest - least * (amount - 1)
    while surplus > 0:
        movable = [i for i in range(1, amount) if holding[i] < largest] or [i for i in range(1, amount) if holding[i] < most]
        mass, left = sum([portions[i] for i in movable]), surplus
        for i in movable:
            extra = min(most - holding[i], max(1, left * portions[i] // mass), surplus)
            holding[i] = holding[i] + extra
            surplus = surplus - extra
    return np.array(holding)


def noise(rng, dims, spread, bound, shards=(), kind=jnp.bfloat16):
    array = jax.random.normal(rng, dims, jnp.float32) * spread
    if len(shards) > 0:
        array = levels(rng, dims, shards, -0.22, 0.18) * array
    return jnp.clip(array, min=-bound, max=bound).astype(kind)


def setup_inputs(seed: int = 0) -> dict:
    splits = jax.random.split(jax.random.key(seed), 8)
    tokens = noise(splits[0], (TOKENS, D), 1.0, 6.0, ((0, 8), (1, 4)))
    output_grad = noise(splits[1], (TOKENS, D), 1.0, 6.0, ((0, 8), (1, 4)))
    route_weight = jnp.clip(jnp.exp(math.log(0.5) - 2.3025851 * jax.random.uniform(splits[2], (TOKENS, TOPK), jnp.float32) ** levels(splits[2], (TOKENS, TOPK), ((0, 8),), -0.2, 0.2)), 0.05, 0.5)
    expert_ids_keys = jax.random.split(jax.random.fold_in(splits[3], 1), TOKENS // TOK_DEV)
    expert_ids_turns = jax.random.permutation(jax.random.fold_in(splits[3], 3), TOKENS // TOK_DEV)
    expert_ids = jax.vmap(lambda own, number: deal_out(jax.random.fold_in(splits[3], 2), own, number, TOK_DEV, EXPERTS, TOPK, CAP, 2))(expert_ids_keys, expert_ids_turns).reshape((TOKENS, TOPK))
    gate_weight = noise(splits[4], (N_EXPERT, D, HALF), D ** -0.5, 0.0625, ((0, 8), (1, 4)))
    up_weight = noise(splits[5], (N_EXPERT, D, HALF), D ** -0.5, 0.0625, ((0, 8), (1, 4)))
    down_weight = noise(splits[6], (N_EXPERT, HALF, D), FF ** -0.5, 0.1875, ((0, 8), (2, 4)))
    return dict(tokens=tokens, output_grad=output_grad, route_weight=route_weight, expert_ids=expert_ids, gate_weight=gate_weight, up_weight=up_weight, down_weight=down_weight)


def block_sum(terms):
    rounded = lax.optimization_barrier(terms.astype(jnp.bfloat16))
    return jnp.sum(rounded.astype(jnp.float32), axis=0)


def expert_pass(rows, grads, gate_w, up_w, down_w):
    slot_count = rows.shape[0]
    hidden_width = gate_w.shape[1]
    slab_width = D // N_FSDP
    row_blocks = rows.astype(jnp.float32).reshape(slot_count, N_FSDP, slab_width)
    grad_blocks = grads.astype(jnp.float32).reshape(slot_count, N_FSDP, slab_width)
    gate_blocks = gate_w.astype(jnp.float32).reshape(N_FSDP, slab_width, hidden_width)
    up_blocks = up_w.astype(jnp.float32).reshape(N_FSDP, slab_width, hidden_width)
    down_blocks = down_w.astype(jnp.float32).reshape(hidden_width, N_FSDP, slab_width)
    highest = lax.Precision.HIGHEST
    gate = block_sum(jnp.einsum("rbd,bdf->brf", row_blocks, gate_blocks, precision=highest))
    up_value = block_sum(jnp.einsum("rbd,bdf->brf", row_blocks, up_blocks, precision=highest))
    hidden_grad = block_sum(jnp.einsum("rbd,fbd->brf", grad_blocks, down_blocks, precision=highest))
    sigmoid_gate = jax.nn.sigmoid(gate)
    activation = (gate * sigmoid_gate * up_value).astype(jnp.bfloat16)
    gate_delta = (hidden_grad * up_value * sigmoid_gate * (1.0 + gate * (1.0 - sigmoid_gate))).astype(jnp.bfloat16)
    up_delta = (hidden_grad * gate * sigmoid_gate).astype(jnp.bfloat16)
    down_grad = jnp.dot(activation.T, grads, preferred_element_type=jnp.float32).astype(jnp.bfloat16)
    gate_grad = jnp.dot(rows.T, gate_delta, preferred_element_type=jnp.float32).astype(jnp.bfloat16)
    up_grad = jnp.dot(rows.T, up_delta, preferred_element_type=jnp.float32).astype(jnp.bfloat16)
    back_rows = jnp.dot(gate_delta, gate_w.T, preferred_element_type=jnp.float32)
    back_rows = back_rows + jnp.dot(up_delta, up_w.T, preferred_element_type=jnp.float32)
    return back_rows.astype(jnp.bfloat16), gate_grad, up_grad, down_grad


def reference(tokens, output_grad, route_weight, expert_ids, gate_weight, up_weight, down_weight):
    slot_count = N_EXPERT * CAP
    in_window = expert_ids < GROUP
    expert_hits = (expert_ids[:, :, None] == jnp.arange(GROUP, dtype=jnp.int32)[None, None, :]).astype(jnp.int32)
    blocked = expert_hits.reshape(N_EXPERT, TOK_DEV * TOPK, GROUP)
    earlier = jnp.cumsum(blocked, axis=1) - blocked
    slot_rank = jnp.sum(earlier * blocked, axis=2).reshape(TOKENS, TOPK).astype(jnp.int32)
    source = (jnp.arange(TOKENS, dtype=jnp.int32) // TOK_DEV)[:, None]
    slot_index = (source * CAP + slot_rank).astype(jnp.int32)
    target = jnp.where(in_window, expert_ids, GROUP).astype(jnp.int32)
    token_index = jnp.broadcast_to(jnp.arange(TOKENS, dtype=jnp.int32)[:, None], (TOKENS, TOPK))
    table = jnp.full((GROUP, slot_count), TOKENS, jnp.int32).at[target, slot_index].set(token_index, mode="drop")
    slot_weight = jnp.zeros((GROUP, slot_count), jnp.float32).at[target, slot_index].set(route_weight, mode="drop")
    table_pairs = jnp.repeat(table, 2, axis=0)
    weight_pairs = jnp.repeat(slot_weight, 2, axis=0)
    padded_tokens = jnp.concatenate([tokens, jnp.zeros((1, D), jnp.bfloat16)], axis=0)
    padded_grads = jnp.concatenate([output_grad, jnp.zeros((1, D), jnp.bfloat16)], axis=0)

    def per_entry(total, inputs):
        rows_index, row_weight, gate_w, up_w, down_w = inputs
        rows = padded_tokens[rows_index]
        grads = (row_weight[:, None] * padded_grads[rows_index].astype(jnp.float32)).astype(jnp.bfloat16)
        back_rows, gate_grad, up_grad, down_grad = expert_pass(rows, grads, gate_w, up_w, down_w)
        total = total.at[rows_index].add(back_rows.astype(jnp.float32))
        return total, (gate_grad, up_grad, down_grad)

    start_total = jnp.zeros((TOKENS + 1, D), jnp.float32)
    total, grads_out = lax.scan(per_entry, start_total, (table_pairs, weight_pairs, gate_weight, up_weight, down_weight))
    gate_grad, up_grad, down_grad = grads_out
    return total[:TOKENS].astype(jnp.bfloat16), gate_grad, up_grad, down_grad
```

```python
import functools

import jax
import jax.numpy as jnp
from jax import lax
from jax.experimental import pallas as pl
from jax.experimental.pallas import tpu as pltpu
from jax.sharding import PartitionSpec as P

CAP = 12
PAIR = 2 * CAP
BF16, F32 = jnp.bfloat16, jnp.float32
OVER_COLUMNS = (((1,), (1,)), ((), ()))
OVER_ROWS = (((0,), (0,)), ((), ()))


def dot(a, b, dims=None):
    if dims is None:
        dims = (((1,), (0,)), ((), ()))
    return lax.dot_general(a, b, dims, preferred_element_type=F32)


def upper(rows, columns):
    shape = (rows // PAIR, PAIR, columns)
    return (lax.broadcasted_iota(jnp.int32, shape, 1) < CAP).reshape(rows, columns)


def swapped(v, first):
    rows = v.shape[0]
    return jnp.where(first, pltpu.roll(v, rows - CAP, 0), pltpu.roll(v, CAP, 0))


def call(kernel, outs, *args, vmem=24, **kw):
    space = pl.BlockSpec(memory_space=pltpu.VMEM)
    return pl.pallas_call(
        kernel,
        out_shape=outs,
        in_specs=[space] * len(args),
        out_specs=jax.tree.map(lambda _: space, outs),
        compiler_params=pltpu.CompilerParams(vmem_limit_bytes=vmem << 20),
        **kw,
    )(*args)


def shape(dims, dtype=BF16):
    return jax.ShapeDtypeStruct(dims, dtype)


def route_kernel(window, e_ref, ids_ref, w_ref, lo_ref, hi_ref, *outs):
    messages, (p0_ref, p1_ref, scale_ref) = outs[:window], outs[window:]
    top, tok = ids_ref.shape
    dims = (window, PAIR, tok)
    rows = window * PAIR
    expert = lax.broadcasted_iota(jnp.int32, dims, 0) + e_ref[0]
    expert = jnp.where(expert >= window, expert - window, expert)
    slot = lax.broadcasted_iota(jnp.int32, dims, 1).astype(F32).reshape(rows, tok)
    hit = jnp.zeros(dims, F32)
    weight = jnp.zeros(dims, F32)
    for k in range(top):
        same = ids_ref[k : k + 1, :][None] == expert
        hit = jnp.where(same, 1.0, hit)
        weight = jnp.where(same, w_ref[k : k + 1, :][None], weight)
    hit = hit.reshape(rows, tok)
    weight = weight.reshape(rows, tok)
    before = lax.broadcasted_iota(jnp.int32, (tok, tok), 0) < lax.broadcasted_iota(
        jnp.int32, (tok, tok), 1
    )
    rank = dot(hit.astype(BF16), before.astype(F32).astype(BF16))
    p0 = jnp.where(rank == slot, hit, 0.0)
    p1 = jnp.where(rank + CAP == slot, hit, 0.0)
    scale_ref[...] = jnp.broadcast_to(
        jnp.sum((p0 + p1) * weight, axis=1, keepdims=True), scale_ref.shape
    )
    p0, p1 = p0.astype(BF16), p1.astype(BF16)
    p0_ref[...] = p0
    p1_ref[...] = p1
    message = dot(p0, lo_ref[...]) + dot(p1, hi_ref[...])
    for d in range(window):
        messages[d][...] = message[d * PAIR : (d + 1) * PAIR].astype(BF16)


def grads_kernel(window, p0_ref, p1_ref, scale_ref, lo_ref, hi_ref, *messages):
    message = dot(p0_ref[...], lo_ref[...]) + dot(p1_ref[...], hi_ref[...])
    message = message * scale_ref[:, 0:1]
    for d in range(window):
        messages[d][...] = message[d * PAIR : (d + 1) * PAIR].astype(BF16)


def joined(refs):
    return jnp.concatenate([r[...].astype(F32) for r in refs], axis=0)


def gate_up_kernel(*refs):
    blocks, gate_ref, up_ref, out_ref = refs[:-3], refs[-3], refs[-2], refs[-1]
    w = blocks[0].shape[1]
    rows = joined(blocks)
    first = upper(*rows.shape)
    turned = swapped(rows, first).astype(BF16)
    rows = rows.astype(BF16)
    gate = dot(rows, gate_ref[0, :w]) + dot(turned, gate_ref[0, w:])
    up = dot(turned, up_ref[0, :w]) + dot(rows, up_ref[0, w:])
    out_ref[...] = jnp.where(upper(*gate.shape), gate, up).astype(BF16)


def hidden_kernel(*refs):
    blocks, down_ref, out_ref = refs[:-2], refs[-2], refs[-1]
    w = blocks[0].shape[1]
    rows = joined(blocks)
    turned = swapped(rows, upper(*rows.shape))
    n = out_ref.shape[0]
    low = jnp.concatenate([rows[:n], turned[n:]], axis=0).astype(BF16)
    high = jnp.concatenate([turned[:n], rows[n:]], axis=0).astype(BF16)
    part = dot(low, down_ref[0, :, :w], OVER_COLUMNS) + dot(high, down_ref[0, :, w:], OVER_COLUMNS)
    out_ref[...] = jnp.where(upper(n, part.shape[1]), part[:n], part[n:]).astype(BF16)


def delta_kernel(gu_a, gu_b, h_a, h_b, gate_ref, up_ref, d_ref, dt_ref, act_ref, back_ref):
    gu = gu_a[...].astype(F32) + gu_b[...].astype(F32)
    h = h_a[...].astype(F32) + h_b[...].astype(F32)
    n = h.shape[0]
    first = upper(*gu.shape)
    half = upper(*h.shape)
    gu_t, h_t = swapped(gu, first), swapped(h, half)
    gate, up = jnp.where(first, gu, gu_t), jnp.where(first, gu_t, gu)
    hidden = jnp.concatenate([jnp.where(half, h, h_t), jnp.where(half, h_t, h)], axis=0)
    sig = jax.nn.sigmoid(gate)
    act_ref[...] = (gate * sig * up).astype(BF16)
    gate_delta = hidden * up * sig * (1.0 + gate * (1.0 - sig))
    up_delta = hidden * gate * sig
    d = jnp.where(first, gate_delta, up_delta).astype(BF16)
    dt = jnp.where(first, up_delta, gate_delta).astype(BF16)
    d_ref[...] = d
    dt_ref[...] = dt
    back_part(d[n:], dt[n:], gate_ref, up_ref, back_ref)


def back_part(d, dt, gate_ref, up_ref, back_ref):
    w = back_ref.shape[1]
    low = dot(d, gate_ref[0, :w], OVER_COLUMNS) + dot(dt, up_ref[0, :w], OVER_COLUMNS)
    high = dot(dt, gate_ref[0, w:], OVER_COLUMNS) + dot(d, up_ref[0, w:], OVER_COLUMNS)
    back_ref[...] = jnp.where(upper(*low.shape), low, high).astype(BF16)


def back_kernel(d_ref, dt_ref, gate_ref, up_ref, back_ref):
    n = back_ref.shape[0]
    back_part(d_ref[:n], dt_ref[:n], gate_ref, up_ref, back_ref)


def gate_up_grad_kernel(*refs):
    blocks, (d_ref, dt_ref, gate_ref, up_ref) = refs[:-4], refs[-4:]
    rows = joined(blocks).astype(BF16)
    first = upper(*d_ref.shape)
    keep = jnp.logical_xor(first, pl.program_id(0) == 1)
    d, dt = d_ref[...].astype(F32), dt_ref[...].astype(F32)
    low = pl.program_id(0) == 0
    gate = jnp.where(keep, jnp.where(low, d, dt), 0.0).astype(BF16)
    up = jnp.where(keep, jnp.where(low, dt, d), 0.0).astype(BF16)
    gate_ref[0] = dot(rows, gate, OVER_ROWS).astype(BF16)
    up_ref[0] = dot(rows, up, OVER_ROWS).astype(BF16)


def down_grad_kernel(*refs):
    blocks, (act_ref, out_ref) = refs[:-2], refs[-2:]
    rows = joined(blocks).astype(BF16)
    keep = jnp.logical_xor(upper(*act_ref.shape), pl.program_id(0) == 1)
    act = jnp.where(keep, act_ref[...].astype(F32), 0.0).astype(BF16)
    out_ref[0] = dot(act, rows, OVER_ROWS).astype(BF16)


def combine_kernel(*refs):
    blocks, (p0_ref, p1_ref, lo_ref, hi_ref) = refs[:-4], refs[-4:]
    rows = joined(blocks).astype(BF16)
    lo_ref[...] = dot(p0_ref[...], rows, OVER_ROWS).astype(BF16)
    hi_ref[...] = dot(p1_ref[...], rows, OVER_ROWS).astype(BF16)


def body(tokens, output_grad, route_weight, expert_ids, gate_weight, up_weight, down_weight):
    expert_count, fsdp_count = lax.axis_size("expert"), lax.axis_size("fsdp")
    window = expert_count // 2
    tok, slab = tokens.shape
    w = slab // 2
    hidden = gate_weight.shape[2]
    rows = window * PAIR
    first_expert = (lax.axis_index("expert") // 2).astype(jnp.int32).reshape(1)

    def shift(v, d):
        perm = [
            (c * 2 + h, ((c + d) % window) * 2 + h) for c in range(window) for h in range(2)
        ]
        return lax.ppermute(v, "expert", perm)

    def other_half(v):
        return lax.ppermute(v, "expert", [(e, e ^ 1) for e in range(expert_count)])

    def fsdp_swap(v, bit):
        return lax.ppermute(v, "fsdp", [(f, f ^ bit) for f in range(fsdp_count)])

    space = pl.BlockSpec(memory_space=pltpu.VMEM)
    smem = pl.BlockSpec(memory_space=pltpu.SMEM)
    params = pltpu.CompilerParams(vmem_limit_bytes=16 << 20)
    message = shape((PAIR, w))
    routed = pl.pallas_call(
        functools.partial(route_kernel, window),
        out_shape=(message,) * window
        + (shape((rows, tok)), shape((rows, tok)), shape((rows, 128), F32)),
        in_specs=[smem] + [space] * 4,
        out_specs=(space,) * (window + 3),
        compiler_params=params,
    )(first_expert, expert_ids.T, route_weight.T, tokens[:, :w], tokens[:, w:])
    row_blocks, (p0, p1, scale) = routed[:window], routed[window:]
    grad_blocks = call(
        functools.partial(grads_kernel, window),
        (message,) * window,
        p0, p1, scale, output_grad[:, :w], output_grad[:, w:],
    )

    def dispatched(blocks):
        own = [blocks[0]] + [shift(blocks[d], d) for d in range(1, window)]
        return own, other_half(jnp.concatenate(own, axis=0))

    own_rows, other_rows = dispatched(row_blocks)
    own_grads, other_grads = dispatched(grad_blocks)

    def reduced(part):
        bit = 1
        while bit * 2 < fsdp_count:
            got = fsdp_swap(part, bit)
            part = (part.astype(F32) + got.astype(F32)).astype(BF16)
            bit *= 2
        return part, fsdp_swap(part, bit)

    gu = call(
        gate_up_kernel, shape((2 * rows, hidden)), *own_rows, other_rows, gate_weight, up_weight
    )
    gu_a, gu_b = reduced(gu)
    part = call(
        hidden_kernel, shape((rows, hidden)), *own_grads, other_grads, down_weight
    )
    h_a, h_b = reduced(part)
    d, dt, act, back_other = call(
        delta_kernel,
        (shape((2 * rows, hidden)),) * 3 + (shape((rows, w)),),
        gu_a, gu_b, h_a, h_b, gate_weight, up_weight,
    )
    returned = other_half(back_other)
    back_own = call(back_kernel, shape((rows, w)), d, dt, gate_weight, up_weight)
    back = (back_own.astype(F32) + returned.astype(F32)).astype(BF16)
    home = [back[:PAIR]] + [
        shift(back[k * PAIR : (k + 1) * PAIR], window - k) for k in range(1, window)
    ]

    def whole(v):
        return pl.BlockSpec(v.shape, lambda i: (0,) * v.ndim)

    grad_args = (*own_rows, other_rows, d, dt)
    gate_grad, up_grad = pl.pallas_call(
        gate_up_grad_kernel,
        grid=(2,),
        out_shape=(shape(gate_weight.shape),) * 2,
        in_specs=[whole(v) for v in grad_args],
        out_specs=(pl.BlockSpec((1, w, hidden), lambda i: (0, i, 0)),) * 2,
        compiler_params=params,
    )(*grad_args)
    down_args = (*own_grads, other_grads, act)
    aligned = w % 128 == 0
    down_grad = pl.pallas_call(
        down_grad_kernel,
        grid=(2,),
        out_shape=shape(down_weight.shape if aligned else (2, hidden, w)),
        in_specs=[whole(v) for v in down_args],
        out_specs=pl.BlockSpec((1, hidden, w), (lambda i: (0, 0, i)) if aligned else (lambda i: (i, 0, 0))),
        compiler_params=params,
    )(*down_args)
    if not aligned:
        down_grad = jnp.concatenate([down_grad[:1], down_grad[1:]], axis=2)
    lo, hi = call(combine_kernel, (shape((tok, w)),) * 2, *home, p0, p1)
    token_grad = jnp.concatenate([lo, hi], axis=1)
    return token_grad, gate_grad, up_grad, down_grad


def solution(mesh):
    placed = (
        P("expert", "fsdp"),
        P("expert", "fsdp"),
        P("expert", None),
        P("expert", None),
        P("expert", "fsdp", None),
        P("expert", "fsdp", None),
        P("expert", None, "fsdp"),
    )
    return jax.shard_map(
        body,
        mesh=mesh,
        in_specs=placed,
        out_specs=(
            P("expert", "fsdp"),
            P("expert", "fsdp", None),
            P("expert", "fsdp", None),
            P("expert", None, "fsdp"),
        ),
        check_vma=False,
    )
```

```python
import functools

import jax
import jax.numpy as jnp
from jax import lax
from jax.experimental import pallas as pl
from jax.experimental.pallas import tpu as pltpu
from jax.sharding import PartitionSpec as P


CAP = 12
PAIR = 2 * CAP
BF16, F32 = jnp.bfloat16, jnp.float32
OVER_COLUMNS = (((1,), (1,)), ((), ()))
OVER_ROWS = (((0,), (0,)), ((), ()))


def dot(a, b, dims=None):
    if dims is None:
        dims = (((1,), (0,)), ((), ()))
    return lax.dot_general(a, b, dims, preferred_element_type=F32)


def upper(rows, columns):
    shape = (rows // PAIR, PAIR, columns)
    return (lax.broadcasted_iota(jnp.int32, shape, 1) < CAP).reshape(rows, columns)


def swapped(v, first):
    rows = v.shape[0]
    return jnp.where(first, pltpu.roll(v, rows - CAP, 0), pltpu.roll(v, CAP, 0))


def call(kernel, outs, *args, vmem=24, **kw):
    space = pl.BlockSpec(memory_space=pltpu.VMEM)
    return pl.pallas_call(
        kernel,
        out_shape=outs,
        in_specs=[space] * len(args),
        out_specs=jax.tree.map(lambda _: space, outs),
        compiler_params=pltpu.CompilerParams(vmem_limit_bytes=vmem << 20),
        **kw,
    )(*args)


def in_hbm(v):
    return pltpu.with_memory_space_constraint(v, pltpu.HBM)


def shape(dims, dtype=BF16):
    return jax.ShapeDtypeStruct(dims, dtype)


def columns(refs):
    if len(refs) == 2:
        return refs
    w = refs[0].shape[1] // 2
    return refs[0].at[:, 0:w], refs[0].at[:, w : 2 * w]


def place_kernel(window, halves, *refs):
    e_ref, ids_hbm, w_hbm = refs[:3]
    sources = columns(refs[3 : 3 + halves]) + columns(refs[3 + halves : 3 + 2 * halves])
    outs = refs[3 + 2 * halves : -4]
    held, ids_ref, w_ref, sems = refs[-4:]
    messages, (p0_ref, p1_ref) = outs[:window], outs[window:]
    copies = [pltpu.make_async_copy(src, dst, sem) for src, dst, sem in zip(
        (ids_hbm, w_hbm) + tuple(sources),
        (ids_ref, w_ref) + tuple(held.at[i] for i in range(4)),
        [sems.at[i] for i in range(6)],
    )]
    for copy in copies:
        copy.start()
    copies[0].wait()
    copies[1].wait()
    top, tok = ids_ref.shape
    dims = (window, PAIR, tok)
    rows = window * PAIR
    expert = lax.broadcasted_iota(jnp.int32, dims, 0) + e_ref[0]
    expert = jnp.where(expert >= window, expert - window, expert)
    slot = lax.broadcasted_iota(jnp.int32, dims, 1).astype(F32).reshape(rows, tok)
    hit = jnp.zeros(dims, F32)
    weight = jnp.zeros(dims, F32)
    for k in range(top):
        same = ids_ref[k : k + 1, :][None] == expert
        hit = jnp.where(same, 1.0, hit)
        weight = jnp.where(same, w_ref[k : k + 1, :][None], weight)
    hit = hit.reshape(rows, tok)
    weight = weight.reshape(rows, tok)
    before = lax.broadcasted_iota(jnp.int32, (tok, tok), 0) < lax.broadcasted_iota(
        jnp.int32, (tok, tok), 1
    )
    rank = dot(hit.astype(BF16), before.astype(F32).astype(BF16))
    p0 = jnp.where(rank == slot, hit, 0.0)
    p1 = jnp.where(rank + CAP == slot, hit, 0.0)
    scale = jnp.sum((p0 + p1) * weight, axis=1, keepdims=True)
    p0, p1 = p0.astype(BF16), p1.astype(BF16)
    p0_ref[...] = p0
    p1_ref[...] = p1
    copies[2].wait()
    copies[3].wait()
    message = dot(p0, held[0]) + dot(p1, held[1])
    for d in range(window):
        messages[d][:PAIR] = message[d * PAIR : (d + 1) * PAIR].astype(BF16)
    copies[4].wait()
    copies[5].wait()
    message = (dot(p0, held[2]) + dot(p1, held[3])) * scale
    for d in range(window):
        messages[d][PAIR:] = message[d * PAIR : (d + 1) * PAIR].astype(BF16)


def load_kernel(*refs):
    n = (len(refs) - 1) // 2
    copies = [pltpu.make_async_copy(refs[i], refs[n + i], refs[-1].at[i]) for i in range(n)]
    for copy in copies:
        copy.start()
    for copy in copies:
        copy.wait()


def joined(refs):
    return jnp.concatenate([r[...].astype(F32) for r in refs], axis=0)


def received(own, other, part):
    take = slice(part * PAIR, (part + 1) * PAIR)
    blocks = [ref[take].astype(F32) for ref in own]
    for d in range(len(own)):
        start = 2 * d * PAIR + part * PAIR
        blocks.append(other[start : start + PAIR].astype(F32))
    return jnp.concatenate(blocks, axis=0)


def product_kernel(count, *refs):
    own, other, (gate_ref, up_ref, down_ref, out_ref) = refs[:count], refs[count], refs[count + 1 :]
    w = other.shape[1]
    n = count * PAIR
    rows = received(own, other, 0)
    first = upper(*rows.shape)
    turned = swapped(rows, first).astype(BF16)
    rows = rows.astype(BF16)
    gate = dot(rows, gate_ref[0, :w]) + dot(turned, gate_ref[0, w:])
    up = dot(turned, up_ref[0, :w]) + dot(rows, up_ref[0, w:])
    out_ref[: 2 * n] = jnp.where(upper(*gate.shape), gate, up).astype(BF16)
    grads = received(own, other, 1)
    turned = swapped(grads, first)
    low = jnp.concatenate([grads[:n], turned[n:]], axis=0).astype(BF16)
    high = jnp.concatenate([turned[:n], grads[n:]], axis=0).astype(BF16)
    part = dot(low, down_ref[0, :, :w], OVER_COLUMNS) + dot(high, down_ref[0, :, w:], OVER_COLUMNS)
    out_ref[2 * n :] = jnp.where(upper(n, part.shape[1]), part[:n], part[n:]).astype(BF16)


def delta_kernel(a_ref, b_ref, gate_ref, up_ref, act_ref, d_ref, dt_ref, own_ref, other_ref):
    n, w = own_ref.shape
    total = a_ref[...].astype(F32) + b_ref[...].astype(F32)
    gu, h = total[: 2 * n], total[2 * n :]
    first = upper(*gu.shape)
    half = upper(*h.shape)
    gu_t, h_t = swapped(gu, first), swapped(h, half)
    gate, up = jnp.where(first, gu, gu_t), jnp.where(first, gu_t, gu)
    hidden = jnp.concatenate([jnp.where(half, h, h_t), jnp.where(half, h_t, h)], axis=0)
    sig = jax.nn.sigmoid(gate)
    act_ref[...] = (gate * sig * up).astype(BF16)
    gate_delta = hidden * up * sig * (1.0 + gate * (1.0 - sig))
    up_delta = hidden * gate * sig
    d = jnp.where(first, gate_delta, up_delta).astype(BF16)
    dt = jnp.where(first, up_delta, gate_delta).astype(BF16)
    d_ref[...] = d
    dt_ref[...] = dt
    low = dot(d, gate_ref[0, :w], OVER_COLUMNS) + dot(dt, up_ref[0, :w], OVER_COLUMNS)
    high = dot(dt, gate_ref[0, w:], OVER_COLUMNS) + dot(d, up_ref[0, w:], OVER_COLUMNS)
    back = jnp.where(upper(*low.shape), low, high).astype(BF16)
    own_ref[...] = back[:n]
    other_ref[...] = back[n:]


def gate_up_grad_kernel(counts, *refs):
    gate_ref, up_ref = refs[-2:]
    low = pl.program_id(0) == 0
    rows, d, dt, at = [], [], [], 0
    for count in counts:
        rows.append(received(refs[at : at + count], refs[at + count], 0))
        at += count + 1
    for i in range(len(counts)):
        d.append(refs[at + 2 * i][...].astype(F32))
        dt.append(refs[at + 2 * i + 1][...].astype(F32))
    rows, d, dt = (jnp.concatenate(v, axis=0) for v in (rows, d, dt))
    rows = rows.astype(BF16)
    keep = jnp.logical_xor(upper(*d.shape), jnp.logical_not(low))
    gate = jnp.where(keep, jnp.where(low, d, dt), 0.0).astype(BF16)
    up = jnp.where(keep, jnp.where(low, dt, d), 0.0).astype(BF16)
    gate_ref[0] = dot(rows, gate, OVER_ROWS).astype(BF16)
    up_ref[0] = dot(rows, up, OVER_ROWS).astype(BF16)


def down_grad_kernel(counts, *refs):
    out_ref = refs[-1]
    grads, act, at = [], [], 0
    for count in counts:
        grads.append(received(refs[at : at + count], refs[at + count], 1))
        at += count + 1
    for i in range(len(counts)):
        act.append(refs[at + i][...].astype(F32))
    grads, act = (jnp.concatenate(v, axis=0) for v in (grads, act))
    keep = jnp.logical_xor(upper(*act.shape), pl.program_id(0) == 1)
    act = jnp.where(keep, act, 0.0).astype(BF16)
    out_ref[0] = dot(act, grads.astype(BF16), OVER_ROWS).astype(BF16)


def combine_kernel(count, *refs):
    blocks, (p0_ref, p1_ref), outs = refs[:count], refs[count : count + 2], refs[count + 2 :]
    rows = joined(blocks).astype(BF16)
    lo_ref, hi_ref = columns(outs)
    lo_ref[...] = dot(p0_ref[...], rows, OVER_ROWS).astype(BF16)
    hi_ref[...] = dot(p1_ref[...], rows, OVER_ROWS).astype(BF16)


def body(tokens, output_grad, route_weight, expert_ids, gate_weight, up_weight, down_weight):
    expert_count, fsdp_count = lax.axis_size("expert"), lax.axis_size("fsdp")
    window = expert_count // 2
    tok, slab = tokens.shape
    w = slab // 2
    aligned = w % 128 == 0
    hidden = gate_weight.shape[2]
    rows = window * PAIR
    first_expert = (lax.axis_index("expert") // 2).astype(jnp.int32).reshape(1)

    def shift(v, d):
        perm = [
            (c * 2 + h, ((c + d) % window) * 2 + h) for c in range(window) for h in range(2)
        ]
        return lax.ppermute(v, "expert", perm)

    def other_half(v):
        return lax.ppermute(v, "expert", [(e, e ^ 1) for e in range(expert_count)])

    def reduced(part):
        bit = 1
        while bit < fsdp_count:
            last = bit * 2 >= fsdp_count
            got = lax.ppermute(part, "fsdp", [(f, f ^ bit) for f in range(fsdp_count)])
            if last:
                return part, got
            part = (part.astype(F32) + got.astype(F32)).astype(BF16)
            bit *= 2

    def halves(v):
        return (v,) if aligned else (v[:, :w], v[:, w:])

    def whole(v):
        return pl.BlockSpec(v.shape, lambda i: (0,) * v.ndim)

    space = pl.BlockSpec(memory_space=pltpu.VMEM)
    smem = pl.BlockSpec(memory_space=pltpu.SMEM)
    hbm = pl.BlockSpec(memory_space=pltpu.HBM)
    params = pltpu.CompilerParams(vmem_limit_bytes=16 << 20)
    message = shape((2 * PAIR, w))
    far = halves(tokens) + halves(output_grad)
    placed = pl.pallas_call(
        functools.partial(place_kernel, window, len(far) // 2),
        out_shape=(message,) * window + (shape((rows, tok)),) * 2,
        in_specs=[smem] + [hbm] * (2 + len(far)),
        out_specs=(space,) * (window + 2),
        scratch_shapes=[
            pltpu.VMEM((4, tok, w), BF16),
            pltpu.VMEM(expert_ids.shape[::-1], jnp.int32),
            pltpu.VMEM(route_weight.shape[::-1], F32),
            pltpu.SemaphoreType.DMA((6,)),
        ],
        compiler_params=params,
    )(first_expert, *(in_hbm(v) for v in (expert_ids.T, route_weight.T, *far)))
    p0, p1 = placed[window:]
    arrived = [placed[0]] + [shift(placed[k], k) for k in range(1, window)]
    weights = (gate_weight, up_weight, down_weight)
    gate_w, up_w, down_w = pl.pallas_call(
        load_kernel,
        out_shape=tuple(shape(v.shape) for v in weights),
        in_specs=[hbm] * 3,
        out_specs=(space,) * 3,
        scratch_shapes=[pltpu.SemaphoreType.DMA((3,))],
        compiler_params=params,
    )(*(in_hbm(v) for v in weights))

    chunks = [range(window // 2), range(window // 2, window)]
    counts = tuple(len(chunk) for chunk in chunks)
    own = [[arrived[d] for d in chunk] for chunk in chunks]
    other = [other_half(jnp.concatenate(v, axis=0)) for v in own]
    sums = []
    for i, count in enumerate(counts):
        part = call(
            functools.partial(product_kernel, count),
            shape((3 * count * PAIR, hidden)),
            *own[i], other[i], gate_w, up_w, down_w,
        )
        sums.append(reduced(part))
    deltas, home = [], []
    for i, count in enumerate(counts):
        n = count * PAIR
        *delta, back_own, back_other = call(
            delta_kernel,
            (shape((2 * n, hidden)),) * 3 + (shape((n, w)),) * 2,
            *sums[i], gate_w, up_w,
        )
        deltas.append(delta)
        returned = other_half(back_other)
        back = (back_own.astype(F32) + returned.astype(F32)).astype(BF16)
        for k, d in enumerate(chunks[i]):
            block = back[k * PAIR : (k + 1) * PAIR]
            home.append(shift(block, window - d) if d else block)

    blocks = tuple(v for i in range(len(chunks)) for v in (*own[i], other[i]))
    grad_args = blocks + tuple(v for delta in deltas for v in delta[1:])
    gate_grad, up_grad = pl.pallas_call(
        functools.partial(gate_up_grad_kernel, counts),
        grid=(2,),
        out_shape=(shape(gate_weight.shape),) * 2,
        in_specs=[whole(v) for v in grad_args],
        out_specs=(pl.BlockSpec((1, w, hidden), lambda i: (0, i, 0)),) * 2,
        compiler_params=params,
    )(*grad_args)
    down_args = blocks + tuple(delta[0] for delta in deltas)
    down_grad = pl.pallas_call(
        functools.partial(down_grad_kernel, counts),
        grid=(2,),
        out_shape=shape(down_weight.shape if aligned else (2, hidden, w)),
        in_specs=[whole(v) for v in down_args],
        out_specs=pl.BlockSpec(
            (1, hidden, w), (lambda i: (0, 0, i)) if aligned else (lambda i: (i, 0, 0))
        ),
        compiler_params=params,
    )(*down_args)
    if not aligned:
        down_grad = jnp.concatenate([down_grad[:1], down_grad[1:]], axis=2)
    out = call(
        functools.partial(combine_kernel, len(home)),
        (shape((tok, slab)),) if aligned else (shape((tok, w)),) * 2,
        *home, p0, p1,
    )
    token_grad = out[0] if aligned else jnp.concatenate(out, axis=1)
    return token_grad, gate_grad, up_grad, down_grad


def solution(mesh):
    placed = (
        P("expert", "fsdp"),
        P("expert", "fsdp"),
        P("expert", None),
        P("expert", None),
        P("expert", "fsdp", None),
        P("expert", "fsdp", None),
        P("expert", None, "fsdp"),
    )
    return jax.shard_map(
        body,
        mesh=mesh,
        in_specs=placed,
        out_specs=(
            P("expert", "fsdp"),
            P("expert", "fsdp", None),
            P("expert", "fsdp", None),
            P("expert", None, "fsdp"),
        ),
        check_vma=False,
    )
```

```python
import functools

import jax
import jax.numpy as jnp
from jax import lax
from jax.experimental import pallas as pl
from jax.experimental.pallas import tpu as pltpu
from jax.sharding import PartitionSpec as P


CAP = 12
PAIR = 2 * CAP
BF16, F32 = jnp.bfloat16, jnp.float32
OVER_COLUMNS = (((1,), (1,)), ((), ()))
OVER_ROWS = (((0,), (0,)), ((), ()))


def dot(a, b, dims=None):
    if dims is None:
        dims = (((1,), (0,)), ((), ()))
    return lax.dot_general(a, b, dims, preferred_element_type=F32)


def upper(rows, columns):
    shape = (rows // PAIR, PAIR, columns)
    return (lax.broadcasted_iota(jnp.int32, shape, 1) < CAP).reshape(rows, columns)


def swapped(v, first):
    rows = v.shape[0]
    return jnp.where(first, pltpu.roll(v, rows - CAP, 0), pltpu.roll(v, CAP, 0))


def call(kernel, outs, *args, vmem=24, **kw):
    space = pl.BlockSpec(memory_space=pltpu.VMEM)
    return pl.pallas_call(
        kernel,
        out_shape=outs,
        in_specs=[space] * len(args),
        out_specs=jax.tree.map(lambda _: space, outs),
        compiler_params=pltpu.CompilerParams(vmem_limit_bytes=vmem << 20),
        **kw,
    )(*args)


def in_hbm(v):
    return pltpu.with_memory_space_constraint(v, pltpu.HBM)


def shape(dims, dtype=BF16):
    return jax.ShapeDtypeStruct(dims, dtype)


def columns(refs):
    if len(refs) == 2:
        return refs
    w = refs[0].shape[1] // 2
    return refs[0].at[:, 0:w], refs[0].at[:, w : 2 * w]


def place_kernel(window, halves, *refs):
    e_ref, ids_hbm, w_hbm = refs[:3]
    sources = columns(refs[3 : 3 + halves]) + columns(refs[3 + halves : 3 + 2 * halves])
    outs = refs[3 + 2 * halves : -4]
    held, ids_ref, w_ref, sems = refs[-4:]
    messages, (p0_ref, p1_ref) = outs[:window], outs[window:]
    copies = [pltpu.make_async_copy(src, dst, sem) for src, dst, sem in zip(
        (ids_hbm, w_hbm) + tuple(sources),
        (ids_ref, w_ref) + tuple(held.at[i] for i in range(4)),
        [sems.at[i] for i in range(6)],
    )]
    for copy in copies:
        copy.start()
    top, tok = ids_ref.shape
    dims = (window, PAIR, tok)
    rows = window * PAIR
    expert = lax.broadcasted_iota(jnp.int32, dims, 0) ^ e_ref[0]
    slot = lax.broadcasted_iota(jnp.int32, dims, 1).astype(F32).reshape(rows, tok)
    before = lax.broadcasted_iota(jnp.int32, (tok, tok), 0) < lax.broadcasted_iota(
        jnp.int32, (tok, tok), 1
    )
    before = before.astype(F32).astype(BF16)
    hit = jnp.zeros(dims, F32)
    weight = jnp.zeros(dims, F32)
    copies[0].wait()
    copies[1].wait()
    for k in range(top):
        same = ids_ref[k : k + 1, :][None] == expert
        hit = jnp.where(same, 1.0, hit)
        weight = jnp.where(same, w_ref[k : k + 1, :][None], weight)
    hit = hit.reshape(rows, tok)
    weight = weight.reshape(rows, tok)
    rank = dot(hit.astype(BF16), before)
    p0 = jnp.where(rank == slot, hit, 0.0)
    p1 = jnp.where(rank + CAP == slot, hit, 0.0)
    scale = jnp.sum((p0 + p1) * weight, axis=1, keepdims=True)
    p0, p1 = p0.astype(BF16), p1.astype(BF16)
    p0_ref[...] = p0
    p1_ref[...] = p1
    copies[2].wait()
    copies[3].wait()
    message = dot(p0, held[0]) + dot(p1, held[1])
    for d in range(window):
        messages[d][:PAIR] = message[d * PAIR : (d + 1) * PAIR].astype(BF16)
    copies[4].wait()
    copies[5].wait()
    message = (dot(p0, held[2]) + dot(p1, held[3])) * scale
    for d in range(window):
        messages[d][PAIR:] = message[d * PAIR : (d + 1) * PAIR].astype(BF16)


def load_kernel(*refs):
    n = (len(refs) - 1) // 2
    copies = [pltpu.make_async_copy(refs[i], refs[n + i], refs[-1].at[i]) for i in range(n)]
    for copy in copies:
        copy.start()
    for copy in copies:
        copy.wait()


def joined(refs):
    return jnp.concatenate([r[...].astype(F32) for r in refs], axis=0)


def received(own, other, part):
    take = slice(part * PAIR, (part + 1) * PAIR)
    blocks = [ref[take].astype(F32) for ref in own]
    for d in range(len(own)):
        start = 2 * d * PAIR + part * PAIR
        blocks.append(other[start : start + PAIR].astype(F32))
    return jnp.concatenate(blocks, axis=0)


def product_kernel(count, *refs):
    own, other, (gate_ref, up_ref, down_ref, out_ref) = refs[:count], refs[count], refs[count + 1 :]
    w = other.shape[1]
    n = count * PAIR
    rows = received(own, other, 0)
    first = upper(*rows.shape)
    turned = swapped(rows, first).astype(BF16)
    rows = rows.astype(BF16)
    gate = dot(rows, gate_ref[0, :w]) + dot(turned, gate_ref[0, w:])
    up = dot(turned, up_ref[0, :w]) + dot(rows, up_ref[0, w:])
    out_ref[: 2 * n] = jnp.where(upper(*gate.shape), gate, up).astype(BF16)
    grads = received(own, other, 1)
    turned = swapped(grads, first)
    low = jnp.concatenate([grads[:n], turned[n:]], axis=0).astype(BF16)
    high = jnp.concatenate([turned[:n], grads[n:]], axis=0).astype(BF16)
    part = dot(low, down_ref[0, :, :w], OVER_COLUMNS) + dot(high, down_ref[0, :, w:], OVER_COLUMNS)
    out_ref[2 * n :] = jnp.where(upper(n, part.shape[1]), part[:n], part[n:]).astype(BF16)


def delta_kernel(a_ref, b_ref, gate_ref, up_ref, act_ref, d_ref, dt_ref, own_ref, other_ref):
    n, w = own_ref.shape
    total = a_ref[...].astype(F32) + b_ref[...].astype(F32)
    gu, h = total[: 2 * n], total[2 * n :]
    first = upper(*gu.shape)
    half = upper(*h.shape)
    gu_t, h_t = swapped(gu, first), swapped(h, half)
    gate, up = jnp.where(first, gu, gu_t), jnp.where(first, gu_t, gu)
    hidden = jnp.concatenate([jnp.where(half, h, h_t), jnp.where(half, h_t, h)], axis=0)
    sig = jax.nn.sigmoid(gate)
    act_ref[...] = (gate * sig * up).astype(BF16)
    gate_delta = hidden * up * sig * (1.0 + gate * (1.0 - sig))
    up_delta = hidden * gate * sig
    d = jnp.where(first, gate_delta, up_delta).astype(BF16)
    dt = jnp.where(first, up_delta, gate_delta).astype(BF16)
    d_ref[...] = d
    dt_ref[...] = dt
    low = dot(d, gate_ref[0, :w], OVER_COLUMNS) + dot(dt, up_ref[0, :w], OVER_COLUMNS)
    high = dot(dt, gate_ref[0, w:], OVER_COLUMNS) + dot(d, up_ref[0, w:], OVER_COLUMNS)
    back = jnp.where(upper(*low.shape), low, high).astype(BF16)
    own_ref[...] = back[:n]
    other_ref[...] = back[n:]


def gate_up_grad_kernel(counts, *refs):
    gate_ref, up_ref = refs[-2:]
    low = pl.program_id(0) == 0
    rows, d, dt, at = [], [], [], 0
    for count in counts:
        rows.append(received(refs[at : at + count], refs[at + count], 0))
        at += count + 1
    for i in range(len(counts)):
        d.append(refs[at + 2 * i][...].astype(F32))
        dt.append(refs[at + 2 * i + 1][...].astype(F32))
    rows, d, dt = (jnp.concatenate(v, axis=0) for v in (rows, d, dt))
    rows = rows.astype(BF16)
    keep = jnp.logical_xor(upper(*d.shape), jnp.logical_not(low))
    gate = jnp.where(keep, jnp.where(low, d, dt), 0.0).astype(BF16)
    up = jnp.where(keep, jnp.where(low, dt, d), 0.0).astype(BF16)
    gate_ref[0] = dot(rows, gate, OVER_ROWS).astype(BF16)
    up_ref[0] = dot(rows, up, OVER_ROWS).astype(BF16)


def down_grad_kernel(counts, *refs):
    out_ref = refs[-1]
    grads, act, at = [], [], 0
    for count in counts:
        grads.append(received(refs[at : at + count], refs[at + count], 1))
        at += count + 1
    for i in range(len(counts)):
        act.append(refs[at + i][...].astype(F32))
    grads, act = (jnp.concatenate(v, axis=0) for v in (grads, act))
    keep = jnp.logical_xor(upper(*act.shape), pl.program_id(0) == 1)
    act = jnp.where(keep, act, 0.0).astype(BF16)
    out_ref[0] = dot(act, grads.astype(BF16), OVER_ROWS).astype(BF16)


def combine_kernel(count, *refs):
    blocks, p_refs = refs[:count], refs[count : count + 2]
    outs, (held, sems) = refs[count + 2 : -2], refs[-2:]
    rows = joined(blocks).astype(BF16)
    copies = []
    for i, (p_ref, out) in enumerate(zip(p_refs, columns(outs))):
        held[i] = dot(p_ref[...], rows, OVER_ROWS).astype(BF16)
        copies.append(pltpu.make_async_copy(held.at[i], out, sems.at[i]))
        copies[-1].start()
    for copy in copies:
        copy.wait()


def body(tokens, output_grad, route_weight, expert_ids, gate_weight, up_weight, down_weight):
    expert_count, fsdp_count = lax.axis_size("expert"), lax.axis_size("fsdp")
    window = expert_count // 2
    tok, slab = tokens.shape
    w = slab // 2
    aligned = w % 128 == 0
    hidden = gate_weight.shape[2]
    rows = window * PAIR
    first_expert = lax.shift_right_logical(lax.axis_index("expert"), 1).reshape(1)

    def across(v, d):
        perm = [(c * 2 + h, (c ^ d) * 2 + h) for c in range(window) for h in range(2)]
        return lax.ppermute(v, "expert", perm)

    def other_half(v):
        return lax.ppermute(v, "expert", [(e, e ^ 1) for e in range(expert_count)])

    def reduced(part):
        bit = 1
        while bit < fsdp_count:
            last = bit * 2 >= fsdp_count
            got = lax.ppermute(part, "fsdp", [(f, f ^ bit) for f in range(fsdp_count)])
            if last:
                return part, got
            part = (part.astype(F32) + got.astype(F32)).astype(BF16)
            bit *= 2

    def halves(v):
        return (v,) if aligned else (v[:, :w], v[:, w:])

    def whole(v):
        return pl.BlockSpec(v.shape, lambda i: (0,) * v.ndim)

    space = pl.BlockSpec(memory_space=pltpu.VMEM)
    smem = pl.BlockSpec(memory_space=pltpu.SMEM)
    hbm = pl.BlockSpec(memory_space=pltpu.HBM)
    params = pltpu.CompilerParams(vmem_limit_bytes=16 << 20)
    message = shape((2 * PAIR, w))
    far = halves(tokens) + halves(output_grad)
    placed = pl.pallas_call(
        functools.partial(place_kernel, window, len(far) // 2),
        out_shape=(message,) * window + (shape((rows, tok)),) * 2,
        in_specs=[smem] + [hbm] * (2 + len(far)),
        out_specs=(space,) * (window + 2),
        scratch_shapes=[
            pltpu.VMEM((4, tok, w), BF16),
            pltpu.VMEM(expert_ids.shape[::-1], jnp.int32),
            pltpu.VMEM(route_weight.shape[::-1], F32),
            pltpu.SemaphoreType.DMA((6,)),
        ],
        compiler_params=params,
    )(first_expert, *(in_hbm(v) for v in (expert_ids.T, route_weight.T, *far)))
    p0, p1 = placed[window:]
    arrived = [placed[0]] + [across(placed[k], k) for k in range(1, window)]
    weights = (up_weight, down_weight)
    up_w, down_w = pl.pallas_call(
        load_kernel,
        out_shape=tuple(shape(v.shape) for v in weights),
        in_specs=[hbm] * 2,
        out_specs=(space,) * 2,
        scratch_shapes=[pltpu.SemaphoreType.DMA((2,))],
        compiler_params=params,
    )(*(in_hbm(v) for v in weights))

    chunks = [range(window // 2), range(window // 2, window)]
    counts = tuple(len(chunk) for chunk in chunks)
    own = [[arrived[d] for d in chunk] for chunk in chunks]
    other = [other_half(jnp.concatenate(v, axis=0)) for v in own]
    sums = []
    for i, count in enumerate(counts):
        part = call(
            functools.partial(product_kernel, count),
            shape((3 * count * PAIR, hidden)),
            *own[i], other[i], gate_weight, up_w, down_w,
        )
        sums.append(reduced(part))
    deltas, home = [], [None] * window
    for i, count in enumerate(counts):
        n = count * PAIR
        *delta, back_own, back_other = call(
            delta_kernel,
            (shape((2 * n, hidden)),) * 3 + (shape((n, w)),) * 2,
            *sums[i], gate_weight, up_w,
        )
        deltas.append(delta)
        returned = other_half(back_other)
        back = (back_own.astype(F32) + returned.astype(F32)).astype(BF16)
        for k, d in enumerate(chunks[i]):
            block = back[k * PAIR : (k + 1) * PAIR]
            home[d] = across(block, d) if d else block

    blocks = tuple(v for i in range(len(chunks)) for v in (*own[i], other[i]))
    grad_args = blocks + tuple(v for delta in deltas for v in delta[1:])
    gate_grad, up_grad = pl.pallas_call(
        functools.partial(gate_up_grad_kernel, counts),
        grid=(2,),
        out_shape=(shape(gate_weight.shape),) * 2,
        in_specs=[whole(v) for v in grad_args],
        out_specs=(pl.BlockSpec((1, w, hidden), lambda i: (0, i, 0)),) * 2,
        compiler_params=params,
    )(*grad_args)
    down_args = blocks + tuple(delta[0] for delta in deltas)
    down_grad = pl.pallas_call(
        functools.partial(down_grad_kernel, counts),
        grid=(2,),
        out_shape=shape(down_weight.shape if aligned else (2, hidden, w)),
        in_specs=[whole(v) for v in down_args],
        out_specs=pl.BlockSpec(
            (1, hidden, w), (lambda i: (0, 0, i)) if aligned else (lambda i: (i, 0, 0))
        ),
        compiler_params=params,
    )(*down_args)
    if not aligned:
        down_grad = jnp.concatenate([down_grad[:1], down_grad[1:]], axis=2)
    out_shape = (shape((tok, slab)),) if aligned else (shape((tok, w)),) * 2
    out = pl.pallas_call(
        functools.partial(combine_kernel, len(home)),
        out_shape=out_shape,
        in_specs=[space] * (len(home) + 2),
        out_specs=(hbm,) * len(out_shape),
        scratch_shapes=[pltpu.VMEM((2, tok, w), BF16), pltpu.SemaphoreType.DMA((2,))],
        compiler_params=params,
    )(*home, p0, p1)
    token_grad = out[0] if aligned else jnp.concatenate(out, axis=1)
    return token_grad, gate_grad, up_grad, down_grad


def solution(mesh):
    placed = (
        P("expert", "fsdp"),
        P("expert", "fsdp"),
        P("expert", None),
        P("expert", None),
        P("expert", "fsdp", None),
        P("expert", "fsdp", None),
        P("expert", None, "fsdp"),
    )
    return jax.shard_map(
        body,
        mesh=mesh,
        in_specs=placed,
        out_specs=(
            P("expert", "fsdp"),
            P("expert", "fsdp", None),
            P("expert", "fsdp", None),
            P("expert", None, "fsdp"),
        ),
        check_vma=False,
    )
```

```python
import functools

import jax
import jax.numpy as jnp
from jax import lax
from jax.experimental import pallas as pl
from jax.experimental.pallas import tpu as pltpu
from jax.sharding import PartitionSpec as P


CAP = 12
PAIR = 2 * CAP
BF16, F32 = jnp.bfloat16, jnp.float32
OVER_COLUMNS = (((1,), (1,)), ((), ()))
OVER_ROWS = (((0,), (0,)), ((), ()))


def dot(a, b, dims=None):
    if dims is None:
        dims = (((1,), (0,)), ((), ()))
    return lax.dot_general(a, b, dims, preferred_element_type=F32)


def upper(rows, columns):
    shape = (rows // PAIR, PAIR, columns)
    return (lax.broadcasted_iota(jnp.int32, shape, 1) < CAP).reshape(rows, columns)


def swapped(v, first):
    rows = v.shape[0]
    return jnp.where(first, pltpu.roll(v, rows - CAP, 0), pltpu.roll(v, CAP, 0))


def call(kernel, outs, *args, vmem=24, **kw):
    space = pl.BlockSpec(memory_space=pltpu.VMEM)
    return pl.pallas_call(
        kernel,
        out_shape=outs,
        in_specs=[space] * len(args),
        out_specs=jax.tree.map(lambda _: space, outs),
        compiler_params=pltpu.CompilerParams(vmem_limit_bytes=vmem << 20),
        **kw,
    )(*args)


def in_hbm(v):
    return pltpu.with_memory_space_constraint(v, pltpu.HBM)


def shape(dims, dtype=BF16):
    return jax.ShapeDtypeStruct(dims, dtype)


def columns(refs):
    if len(refs) == 2:
        return refs
    w = refs[0].shape[1] // 2
    return refs[0].at[:, 0:w], refs[0].at[:, w : 2 * w]


def place_kernel(window, halves, *refs):
    e_ref, ids_hbm, w_hbm = refs[:3]
    sources = columns(refs[3 : 3 + halves]) + columns(refs[3 + halves : 3 + 2 * halves])
    outs = refs[3 + 2 * halves : -4]
    held, ids_ref, w_ref, sems = refs[-4:]
    messages, (p0_ref, p1_ref) = outs[:window], outs[window:]
    copies = [pltpu.make_async_copy(src, dst, sem) for src, dst, sem in zip(
        (ids_hbm, w_hbm) + tuple(sources),
        (ids_ref, w_ref) + tuple(held.at[i] for i in range(4)),
        [sems.at[i] for i in range(6)],
    )]
    for copy in copies:
        copy.start()
    top, tok = ids_ref.shape
    dims = (window, PAIR, tok)
    rows = window * PAIR
    expert = lax.broadcasted_iota(jnp.int32, dims, 0) ^ e_ref[0]
    slot = lax.broadcasted_iota(jnp.int32, dims, 1).astype(F32).reshape(rows, tok)
    before = lax.broadcasted_iota(jnp.int32, (tok, tok), 0) < lax.broadcasted_iota(
        jnp.int32, (tok, tok), 1
    )
    before = before.astype(F32).astype(BF16)
    hit = jnp.zeros(dims, F32)
    weight = jnp.zeros(dims, F32)
    copies[0].wait()
    copies[1].wait()
    for k in range(top):
        same = ids_ref[k : k + 1, :][None] == expert
        hit = jnp.where(same, 1.0, hit)
        weight = jnp.where(same, w_ref[k : k + 1, :][None], weight)
    hit = hit.reshape(rows, tok)
    weight = weight.reshape(rows, tok)
    rank = dot(hit.astype(BF16), before)
    p0 = jnp.where(rank == slot, hit, 0.0)
    p1 = jnp.where(rank + CAP == slot, hit, 0.0)
    scale = jnp.sum((p0 + p1) * weight, axis=1, keepdims=True)
    p0, p1 = p0.astype(BF16), p1.astype(BF16)
    p0_ref[...] = p0
    p1_ref[...] = p1
    copies[2].wait()
    copies[3].wait()
    message = dot(p0, held[0]) + dot(p1, held[1])
    for d in range(window):
        messages[d][:PAIR] = message[d * PAIR : (d + 1) * PAIR].astype(BF16)
    copies[4].wait()
    copies[5].wait()
    message = (dot(p0, held[2]) + dot(p1, held[3])) * scale
    for d in range(window):
        messages[d][PAIR:] = message[d * PAIR : (d + 1) * PAIR].astype(BF16)


def load_kernel(*refs):
    n = (len(refs) - 1) // 2
    copies = [pltpu.make_async_copy(refs[i], refs[n + i], refs[-1].at[i]) for i in range(n)]
    for copy in copies:
        copy.start()
    for copy in copies:
        copy.wait()


def joined(refs):
    return jnp.concatenate([r[...].astype(F32) for r in refs], axis=0)


def received(own, other, part):
    take = slice(part * PAIR, (part + 1) * PAIR)
    blocks = [ref[take].astype(F32) for ref in own]
    for d in range(len(own)):
        start = 2 * d * PAIR + part * PAIR
        blocks.append(other[start : start + PAIR].astype(F32))
    return jnp.concatenate(blocks, axis=0)


def unfolded(v):
    first = upper(*v.shape)
    turned = swapped(v, first)
    low, high = jnp.where(first, v, turned), jnp.where(first, turned, v)
    return jnp.concatenate([low.astype(BF16), high.astype(BF16)], axis=1)


def gate_up_kernel(count, *refs):
    own, other, (gate_ref, up_ref, out_ref) = refs[:count], refs[count], refs[count + 1 :]
    rows = unfolded(received(own, other, 0))
    gate, up = dot(rows, gate_ref[0]), dot(rows, up_ref[0])
    out_ref[: gate.shape[0]] = jnp.where(upper(*gate.shape), gate, up).astype(BF16)


def hidden_kernel(count, *refs):
    own, other, (down_ref, out_ref) = refs[:count], refs[count], refs[count + 1 :]
    n = count * PAIR
    grads = unfolded(received(own, other, 1))
    part = dot(grads, down_ref[0], OVER_COLUMNS)
    start = out_ref.shape[0] - n
    out_ref[start:] = jnp.where(upper(n, part.shape[1]), part[:n], part[n:]).astype(BF16)


def product_kernel(count, *refs):
    blocks, (gate_ref, up_ref, down_ref, out_ref) = refs[: count + 1], refs[count + 1 :]
    gate_up_kernel(count, *blocks, gate_ref, up_ref, out_ref)
    hidden_kernel(count, *blocks, down_ref, out_ref)


def delta_kernel(pairs, sizes, *refs):
    sums, refs = refs[: 2 * pairs], refs[2 * pairs :]
    (gate_ref, up_ref, act_ref, gd_ref, ud_ref), backs = refs[:5], refs[5:]
    n, w = act_ref.shape[0] // 2, backs[0].shape[1]
    totals = [
        sums[2 * i][...].astype(F32) + sums[2 * i + 1][...].astype(F32) for i in range(pairs)
    ]
    gu, h = totals if pairs == 2 else (totals[0][: 2 * n], totals[0][2 * n :])
    first = upper(*gu.shape)
    half = upper(*h.shape)
    gu_t, h_t = swapped(gu, first), swapped(h, half)
    gate, up = jnp.where(first, gu, gu_t), jnp.where(first, gu_t, gu)
    hidden = jnp.concatenate([jnp.where(half, h, h_t), jnp.where(half, h_t, h)], axis=0)
    sig = jax.nn.sigmoid(gate)
    act_ref[...] = (gate * sig * up).astype(BF16)
    gate_delta = hidden * up * sig * (1.0 + gate * (1.0 - sig))
    up_delta = hidden * gate * sig
    gate_delta, up_delta = gate_delta.astype(BF16), up_delta.astype(BF16)
    gd_ref[...] = gate_delta
    ud_ref[...] = up_delta
    back = dot(gate_delta, gate_ref[0], OVER_COLUMNS) + dot(up_delta, up_ref[0], OVER_COLUMNS)
    back = jnp.where(upper(2 * n, w), back[:, :w], back[:, w:]).astype(BF16)
    for i, (start, size) in enumerate(sizes):
        backs[2 * i][...] = back[start : start + size]
        backs[2 * i + 1][...] = back[n + start : n + start + size]


def all_received(counts, refs, part):
    blocks, at = [], 0
    for count in counts:
        blocks.append(received(refs[at : at + count], refs[at + count], part))
        at += count + 1
    return jnp.concatenate(blocks, axis=0), refs[at:]


def gate_up_grad_kernel(counts, *refs):
    rows, refs = all_received(counts, refs, 0)
    k = len(counts)
    deltas = [jnp.concatenate([r[...].astype(F32) for r in refs[i * k : i * k + k]], axis=0) for i in (0, 1)]
    outs, (held, sems) = refs[2 * k : -2], refs[-2:]
    w = rows.shape[1]
    first = upper(*deltas[0].shape)
    turned = rows.T.astype(BF16)
    copies = []
    for half in (0, 1):
        keep = first if half == 0 else jnp.logical_not(first)
        for i, delta in enumerate(deltas):
            at = 2 * half + i
            held[at] = dot(turned, jnp.where(keep, delta, 0.0).astype(BF16)).astype(BF16)
            copies.append(
                pltpu.make_async_copy(
                    held.at[at], outs[i].at[0, half * w : (half + 1) * w], sems.at[at]
                )
            )
            copies[-1].start()
    for copy in copies:
        copy.wait()


def down_grad_kernel(counts, *refs):
    grads, refs = all_received(counts, refs, 1)
    k = len(counts)
    act = jnp.concatenate([r[...].astype(F32) for r in refs[:k]], axis=0)
    outs, (held, sems) = refs[k:-2], refs[-2:]
    w = grads.shape[1]
    grads = grads.astype(BF16)
    first = upper(*act.shape)
    copies = []
    for half in (0, 1):
        keep = first if half == 0 else jnp.logical_not(first)
        held[half] = dot(jnp.where(keep, act, 0.0).astype(BF16), grads, OVER_ROWS).astype(BF16)
        out = outs[0].at[0, :, half * w : (half + 1) * w] if len(outs) == 1 else outs[half].at[0]
        copies.append(pltpu.make_async_copy(held.at[half], out, sems.at[half]))
        copies[-1].start()
    for copy in copies:
        copy.wait()


def early_kernel(count, *refs):
    blocks, (p0_ref, p1_ref, total_ref) = refs[:count], refs[count:]
    rows = joined(blocks).astype(BF16)
    n = rows.shape[0]
    total_ref[0] = dot(p0_ref[:n], rows, OVER_ROWS)
    total_ref[1] = dot(p1_ref[:n], rows, OVER_ROWS)


def combine_kernel(count, *refs):
    blocks, (p0_ref, p1_ref, total_ref) = refs[:count], refs[count : count + 3]
    outs, (held, sems) = refs[count + 3 : -2], refs[-2:]
    rows = joined(blocks).astype(BF16)
    start = p0_ref.shape[0] - rows.shape[0]
    copies = []
    for i, (p_ref, out) in enumerate(zip((p0_ref, p1_ref), columns(outs))):
        held[i] = (total_ref[i] + dot(p_ref[start:], rows, OVER_ROWS)).astype(BF16)
        copies.append(pltpu.make_async_copy(held.at[i], out, sems.at[i]))
        copies[-1].start()
    for copy in copies:
        copy.wait()


def body(tokens, output_grad, route_weight, expert_ids, gate_weight, up_weight, down_weight):
    expert_count, fsdp_count = lax.axis_size("expert"), lax.axis_size("fsdp")
    window = expert_count // 2
    tok, slab = tokens.shape
    w = slab // 2
    aligned = w % 128 == 0
    hidden = gate_weight.shape[2]
    rows = window * PAIR
    first_expert = lax.shift_right_logical(lax.axis_index("expert"), 1).reshape(1)

    def across(v, d):
        perm = [(c * 2 + h, (c ^ d) * 2 + h) for c in range(window) for h in range(2)]
        return lax.ppermute(v, "expert", perm)

    def other_half(v):
        return lax.ppermute(v, "expert", [(e, e ^ 1) for e in range(expert_count)])

    def reduced(part):
        bit = 1
        while bit < fsdp_count:
            last = bit * 2 >= fsdp_count
            got = lax.ppermute(part, "fsdp", [(f, f ^ bit) for f in range(fsdp_count)])
            if last:
                return part, got
            part = (part.astype(F32) + got.astype(F32)).astype(BF16)
            bit *= 2

    def halves(v):
        return (v,) if aligned else (v[:, :w], v[:, w:])

    space = pl.BlockSpec(memory_space=pltpu.VMEM)
    smem = pl.BlockSpec(memory_space=pltpu.SMEM)
    hbm = pl.BlockSpec(memory_space=pltpu.HBM)
    params = pltpu.CompilerParams(vmem_limit_bytes=16 << 20)
    message = shape((2 * PAIR, w))
    far = halves(tokens) + halves(output_grad)
    placed = pl.pallas_call(
        functools.partial(place_kernel, window, len(far) // 2),
        out_shape=(message,) * window + (shape((rows, tok)),) * 2,
        in_specs=[smem] + [hbm] * (2 + len(far)),
        out_specs=(space,) * (window + 2),
        scratch_shapes=[
            pltpu.VMEM((4, tok, w), BF16),
            pltpu.VMEM(expert_ids.shape[::-1], jnp.int32),
            pltpu.VMEM(route_weight.shape[::-1], F32),
            pltpu.SemaphoreType.DMA((6,)),
        ],
        compiler_params=params,
    )(first_expert, *(in_hbm(v) for v in (expert_ids.T, route_weight.T, *far)))
    p0, p1 = placed[window:]
    arrived = [placed[0]] + [across(placed[k], k) for k in range(1, window)]
    weights = (up_weight, down_weight)
    up_w, down_w = pl.pallas_call(
        load_kernel,
        out_shape=tuple(shape(v.shape) for v in weights),
        in_specs=[hbm] * 2,
        out_specs=(space,) * 2,
        scratch_shapes=[pltpu.SemaphoreType.DMA((2,))],
        compiler_params=params,
    )(*(in_hbm(v) for v in weights))

    chunks = [range(window // 2), range(window // 2, window)]
    counts = tuple(len(chunk) for chunk in chunks)
    own = [[arrived[d] for d in chunk] for chunk in chunks]
    other = [other_half(jnp.concatenate(v, axis=0)) for v in own]
    sums = []
    for i, count in enumerate(counts):
        n = count * PAIR
        take = (*own[i], other[i])
        if i == 0:
            part = call(
                functools.partial(product_kernel, count),
                shape((3 * n, hidden)),
                *take, gate_weight, up_w, down_w,
            )
            sums.append(reduced(part))
            continue
        part = call(
            functools.partial(gate_up_kernel, count),
            shape((2 * n, hidden)),
            *take, gate_weight, up_w,
        )
        h_part = call(functools.partial(hidden_kernel, count), shape((n, hidden)), *take, down_w)
        sums.append(reduced(part) + reduced(h_part))
    deltas, home = [], [None] * window
    for i, count in enumerate(counts):
        n = count * PAIR
        chunk = list(chunks[i])
        pieces = [chunk] if i == 0 else [chunk[count // 2 :], chunk[: count // 2]]
        sizes = [((piece[0] - chunk[0]) * PAIR, len(piece) * PAIR) for piece in pieces]
        *delta, = call(
            functools.partial(delta_kernel, len(sums[i]) // 2, sizes),
            (shape((2 * n, hidden)),) * 3
            + tuple(shape((size, w)) for _, size in sizes for _ in range(2)),
            *sums[i], gate_weight, up_w,
        )
        deltas.append(delta[:3])
        for j, piece in enumerate(pieces):
            back_own, back_other = delta[3 + 2 * j], delta[4 + 2 * j]
            returned = other_half(back_other)
            back = (back_own.astype(F32) + returned.astype(F32)).astype(BF16)
            for k, d in enumerate(piece):
                block = back[k * PAIR : (k + 1) * PAIR]
                home[d] = across(block, d) if d else block

    blocks = tuple(v for i in range(len(chunks)) for v in (*own[i], other[i]))
    grad_args = blocks + tuple(delta[i] for i in (1, 2) for delta in deltas)
    gate_grad, up_grad = pl.pallas_call(
        functools.partial(gate_up_grad_kernel, counts),
        out_shape=(shape(gate_weight.shape),) * 2,
        in_specs=[space] * len(grad_args),
        out_specs=(hbm,) * 2,
        scratch_shapes=[pltpu.VMEM((4, w, hidden), BF16), pltpu.SemaphoreType.DMA((4,))],
        compiler_params=params,
    )(*grad_args)
    down_args = blocks + tuple(delta[0] for delta in deltas)
    out_shape = (shape(down_weight.shape),) if aligned else (shape((1, hidden, w)),) * 2
    down_grad = pl.pallas_call(
        functools.partial(down_grad_kernel, counts),
        out_shape=out_shape,
        in_specs=[space] * len(down_args),
        out_specs=(hbm,) * len(out_shape),
        scratch_shapes=[pltpu.VMEM((2, hidden, w), BF16), pltpu.SemaphoreType.DMA((2,))],
        compiler_params=params,
    )(*down_args)
    down_grad = down_grad[0] if aligned else jnp.concatenate(down_grad, axis=2)
    early, late = [home[d] for d in chunks[0]], [home[d] for d in chunks[1]]
    total = call(
        functools.partial(early_kernel, len(early)), shape((2, tok, w), F32), *early, p0, p1
    )
    out_shape = (shape((tok, slab)),) if aligned else (shape((tok, w)),) * 2
    out = pl.pallas_call(
        functools.partial(combine_kernel, len(late)),
        out_shape=out_shape,
        in_specs=[space] * (len(late) + 3),
        out_specs=(hbm,) * len(out_shape),
        scratch_shapes=[pltpu.VMEM((2, tok, w), BF16), pltpu.SemaphoreType.DMA((2,))],
        compiler_params=params,
    )(*late, p0, p1, total)
    token_grad = out[0] if aligned else jnp.concatenate(out, axis=1)
    return token_grad, gate_grad, up_grad, down_grad


def solution(mesh):
    placed = (
        P("expert", "fsdp"),
        P("expert", "fsdp"),
        P("expert", None),
        P("expert", None),
        P("expert", "fsdp", None),
        P("expert", "fsdp", None),
        P("expert", None, "fsdp"),
    )
    return jax.shard_map(
        body,
        mesh=mesh,
        in_specs=placed,
        out_specs=(
            P("expert", "fsdp"),
            P("expert", "fsdp", None),
            P("expert", "fsdp", None),
            P("expert", None, "fsdp"),
        ),
        check_vma=False,
    )
```

```python
import functools

import jax
import jax.numpy as jnp
from jax import lax
from jax.experimental import pallas as pl
from jax.experimental.pallas import tpu as pltpu
from jax.sharding import PartitionSpec as P


CAP = 12
PAIR = 2 * CAP
BF16, F32 = jnp.bfloat16, jnp.float32
OVER_ROWS = (((0,), (0,)), ((), ()))


def dot(a, b, dims=None):
    if dims is None:
        dims = (((1,), (0,)), ((), ()))
    return lax.dot_general(a, b, dims, preferred_element_type=F32)


def upper(rows, columns):
    shape = (rows // PAIR, PAIR, columns)
    return (lax.broadcasted_iota(jnp.int32, shape, 1) < CAP).reshape(rows, columns)


def swapped(v, first):
    rows = v.shape[0]
    return jnp.where(first, pltpu.roll(v, rows - CAP, 0), pltpu.roll(v, CAP, 0))


def call(kernel, outs, *args, vmem=24, **kw):
    space = pl.BlockSpec(memory_space=pltpu.VMEM)
    return pl.pallas_call(
        kernel,
        out_shape=outs,
        in_specs=[space] * len(args),
        out_specs=jax.tree.map(lambda _: space, outs),
        compiler_params=pltpu.CompilerParams(vmem_limit_bytes=vmem << 20),
        **kw,
    )(*args)


def in_hbm(v):
    return pltpu.with_memory_space_constraint(v, pltpu.HBM)


def shape(dims, dtype=BF16):
    return jax.ShapeDtypeStruct(dims, dtype)


def columns(refs):
    if len(refs) == 2:
        return refs
    w = refs[0].shape[1] // 2
    return refs[0].at[:, 0:w], refs[0].at[:, w : 2 * w]


def place_kernel(window, halves, *refs):
    e_ref, ids_hbm, w_hbm = refs[:3]
    sources = columns(refs[3 : 3 + halves]) + columns(refs[3 + halves : 3 + 2 * halves])
    outs = refs[3 + 2 * halves : -4]
    held, ids_ref, w_ref, sems = refs[-4:]
    messages, (p0_ref, p1_ref) = outs[:window], outs[window:]
    top, tok = ids_ref.shape
    copies = [pltpu.make_async_copy(src, dst, sem) for src, dst, sem in zip(
        (ids_hbm, w_hbm) + tuple(sources),
        (ids_ref, w_ref) + tuple(held.at[i // 2, tok * (i % 2) : tok * (i % 2 + 1)] for i in range(4)),
        [sems.at[i] for i in range(6)],
    )]
    for copy in copies:
        copy.start()
    top, tok = ids_ref.shape
    dims = (window, PAIR, tok)
    rows = window * PAIR
    expert = lax.broadcasted_iota(jnp.int32, dims, 0) ^ e_ref[0]
    slot = lax.broadcasted_iota(jnp.int32, dims, 1).astype(F32).reshape(rows, tok)
    before = lax.broadcasted_iota(jnp.int32, (tok, tok), 0) < lax.broadcasted_iota(
        jnp.int32, (tok, tok), 1
    )
    before = before.astype(F32).astype(BF16)
    hit = jnp.zeros(dims, F32)
    weight = jnp.zeros(dims, F32)
    copies[0].wait()
    copies[1].wait()
    for k in range(top):
        same = ids_ref[k : k + 1, :][None] == expert
        hit = jnp.where(same, 1.0, hit)
        weight = jnp.where(same, w_ref[k : k + 1, :][None], weight)
    hit = hit.reshape(rows, tok)
    weight = weight.reshape(rows, tok)
    rank = dot(hit.astype(BF16), before)
    p0 = jnp.where(rank == slot, hit, 0.0)
    p1 = jnp.where(rank + CAP == slot, hit, 0.0)
    scale = jnp.sum((p0 + p1) * weight, axis=1, keepdims=True)
    p0, p1 = p0.astype(BF16), p1.astype(BF16)
    p0_ref[...] = p0
    p1_ref[...] = p1
    both = jnp.concatenate([p0, p1], axis=1)
    copies[2].wait()
    copies[3].wait()
    message = dot(both, held[0])
    for d in range(window):
        messages[d][:PAIR] = message[d * PAIR : (d + 1) * PAIR].astype(BF16)
    copies[4].wait()
    copies[5].wait()
    message = dot(both, held[1]) * scale
    for d in range(window):
        messages[d][PAIR:] = message[d * PAIR : (d + 1) * PAIR].astype(BF16)


def load_kernel(gate_ref, up_hbm, down_hbm, up_ref, gate_t, up_t, down_t, down_ref, sems):
    up_copy = pltpu.make_async_copy(up_hbm, up_ref, sems.at[0])
    down_copy = pltpu.make_async_copy(down_hbm, down_ref, sems.at[1])
    up_copy.start()
    down_copy.start()
    gate_t[...] = gate_ref[0].T
    up_copy.wait()
    up_t[...] = up_ref[0].T
    down_copy.wait()
    down_t[...] = down_ref[0].T


def joined(refs):
    return jnp.concatenate([r[...].astype(F32) for r in refs], axis=0)


def received(own, other, part):
    take = slice(part * PAIR, (part + 1) * PAIR)
    blocks = [ref[take].astype(F32) for ref in own]
    for d in range(len(own)):
        start = 2 * d * PAIR + part * PAIR
        blocks.append(other[start : start + PAIR].astype(F32))
    return jnp.concatenate(blocks, axis=0)


def unfolded(v):
    first = upper(*v.shape)
    turned = swapped(v, first)
    low, high = jnp.where(first, v, turned), jnp.where(first, turned, v)
    return jnp.concatenate([low.astype(BF16), high.astype(BF16)], axis=1)


def gate_up_kernel(count, *refs):
    own, other, (gate_ref, up_ref, out_ref) = refs[:count], refs[count], refs[count + 1 :]
    rows = unfolded(received(own, other, 0))
    gate, up = dot(rows, gate_ref[0]), dot(rows, up_ref[0])
    out_ref[: gate.shape[0]] = jnp.where(upper(*gate.shape), gate, up).astype(BF16)


def hidden_kernel(count, *refs):
    own, other, (down_ref, out_ref) = refs[:count], refs[count], refs[count + 1 :]
    n = count * PAIR
    grads = unfolded(received(own, other, 1))
    part = dot(grads, down_ref[...])
    start = out_ref.shape[0] - n
    out_ref[start:] = jnp.where(upper(n, part.shape[1]), part[:n], part[n:]).astype(BF16)


def product_kernel(count, *refs):
    blocks, (gate_ref, up_ref, down_ref, out_ref) = refs[: count + 1], refs[count + 1 :]
    gate_up_kernel(count, *blocks, gate_ref, up_ref, out_ref)
    hidden_kernel(count, *blocks, down_ref, out_ref)


def delta_kernel(pairs, sizes, *refs):
    sums, refs = refs[: 2 * pairs], refs[2 * pairs :]
    (gate_ref, up_ref, act_ref, gd_ref, ud_ref), backs = refs[:5], refs[5:]
    n, w = act_ref.shape[0] // 2, backs[0].shape[1]
    totals = [
        sums[2 * i][...].astype(F32) + sums[2 * i + 1][...].astype(F32) for i in range(pairs)
    ]
    gu, h = totals if pairs == 2 else (totals[0][: 2 * n], totals[0][2 * n :])
    first = upper(*gu.shape)
    half = upper(*h.shape)
    gu_t, h_t = swapped(gu, first), swapped(h, half)
    gate, up = jnp.where(first, gu, gu_t), jnp.where(first, gu_t, gu)
    hidden = jnp.concatenate([jnp.where(half, h, h_t), jnp.where(half, h_t, h)], axis=0)
    sig = jax.nn.sigmoid(gate)
    act_ref[...] = (gate * sig * up).astype(BF16)
    gate_delta = hidden * up * sig * (1.0 + gate * (1.0 - sig))
    up_delta = hidden * gate * sig
    gate_delta, up_delta = gate_delta.astype(BF16), up_delta.astype(BF16)
    gd_ref[...] = gate_delta
    ud_ref[...] = up_delta
    back = dot(gate_delta, gate_ref[...]) + dot(up_delta, up_ref[...])
    back = jnp.where(upper(2 * n, w), back[:, :w], back[:, w:]).astype(BF16)
    for i, (start, size) in enumerate(sizes):
        backs[2 * i][...] = back[start : start + size]
        backs[2 * i + 1][...] = back[n + start : n + start + size]


def all_received(counts, refs, part):
    blocks, at = [], 0
    for count in counts:
        blocks.append(received(refs[at : at + count], refs[at + count], part))
        at += count + 1
    return jnp.concatenate(blocks, axis=0), refs[at:]


def gate_up_grad_kernel(counts, *refs):
    rows, refs = all_received(counts, refs, 0)
    k = len(counts)
    deltas = [jnp.concatenate([r[...].astype(F32) for r in refs[i * k : i * k + k]], axis=0) for i in (0, 1)]
    outs, (held, sems) = refs[2 * k : -2], refs[-2:]
    w = rows.shape[1]
    first = upper(*deltas[0].shape)
    turned = rows.T.astype(BF16)
    copies = []
    for half in (0, 1):
        keep = first if half == 0 else jnp.logical_not(first)
        for i, delta in enumerate(deltas):
            at = 2 * half + i
            held[at] = dot(turned, jnp.where(keep, delta, 0.0).astype(BF16)).astype(BF16)
            copies.append(
                pltpu.make_async_copy(
                    held.at[at], outs[i].at[0, half * w : (half + 1) * w], sems.at[at]
                )
            )
            copies[-1].start()
    for copy in copies:
        copy.wait()


def down_grad_kernel(counts, *refs):
    grads, refs = all_received(counts, refs, 1)
    k = len(counts)
    act = jnp.concatenate([r[...].astype(F32) for r in refs[:k]], axis=0)
    outs, (held, sems) = refs[k:-2], refs[-2:]
    w = grads.shape[1]
    grads = grads.astype(BF16)
    first = upper(*act.shape)
    copies = []
    for half in (0, 1):
        keep = first if half == 0 else jnp.logical_not(first)
        held[half] = dot(jnp.where(keep, act, 0.0).astype(BF16), grads, OVER_ROWS).astype(BF16)
        out = outs[0].at[0, :, half * w : (half + 1) * w] if len(outs) == 1 else outs[half].at[0]
        copies.append(pltpu.make_async_copy(held.at[half], out, sems.at[half]))
        copies[-1].start()
    for copy in copies:
        copy.wait()


def combine_kernel(count, *refs):
    blocks, (p0_ref, p1_ref) = refs[:count], refs[count : count + 2]
    outs, (held, sems) = refs[count + 2 : -2], refs[-2:]
    rows = joined(blocks).astype(BF16)
    copies = []
    tok = p0_ref.shape[1]
    for k in range(2):
        here = slice(k * tok // 2, (k + 1) * tok // 2)
        for i, (p_ref, out) in enumerate(zip((p0_ref, p1_ref), columns(outs))):
            held[i, here] = dot(p_ref[:, here], rows, OVER_ROWS).astype(BF16)
            copies.append(
                pltpu.make_async_copy(held.at[i, here], out.at[here], sems.at[2 * k + i])
            )
            copies[-1].start()
    for copy in copies:
        copy.wait()


def body(tokens, output_grad, route_weight, expert_ids, gate_weight, up_weight, down_weight):
    expert_count, fsdp_count = lax.axis_size("expert"), lax.axis_size("fsdp")
    window = expert_count // 2
    tok, slab = tokens.shape
    w = slab // 2
    aligned = w % 128 == 0
    hidden = gate_weight.shape[2]
    rows = window * PAIR
    first_expert = lax.shift_right_logical(lax.axis_index("expert"), 1).reshape(1)

    def across(v, d):
        perm = [(c * 2 + h, (c ^ d) * 2 + h) for c in range(window) for h in range(2)]
        return lax.ppermute(v, "expert", perm)

    def other_half(v):
        return lax.ppermute(v, "expert", [(e, e ^ 1) for e in range(expert_count)])

    def reduced(part):
        bit = 1
        while bit < fsdp_count:
            last = bit * 2 >= fsdp_count
            got = lax.ppermute(part, "fsdp", [(f, f ^ bit) for f in range(fsdp_count)])
            if last:
                return part, got
            part = (part.astype(F32) + got.astype(F32)).astype(BF16)
            bit *= 2

    def halves(v):
        return (v,) if aligned else (v[:, :w], v[:, w:])

    space = pl.BlockSpec(memory_space=pltpu.VMEM)
    smem = pl.BlockSpec(memory_space=pltpu.SMEM)
    hbm = pl.BlockSpec(memory_space=pltpu.HBM)
    params = pltpu.CompilerParams(vmem_limit_bytes=16 << 20)
    message = shape((2 * PAIR, w))
    far = halves(tokens) + halves(output_grad)
    placed = pl.pallas_call(
        functools.partial(place_kernel, window, len(far) // 2),
        out_shape=(message,) * window + (shape((rows, tok)),) * 2,
        in_specs=[smem] + [hbm] * (2 + len(far)),
        out_specs=(space,) * (window + 2),
        scratch_shapes=[
            pltpu.VMEM((2, 2 * tok, w), BF16),
            pltpu.VMEM(expert_ids.shape[::-1], jnp.int32),
            pltpu.VMEM(route_weight.shape[::-1], F32),
            pltpu.SemaphoreType.DMA((6,)),
        ],
        compiler_params=params,
    )(first_expert, *(in_hbm(v) for v in (expert_ids.T, route_weight.T, *far)))
    p0, p1 = placed[window:]
    arrived = [placed[0]] + [across(placed[k], k) for k in range(1, window)]
    up_w, gate_t, up_t, down_t = pl.pallas_call(
        load_kernel,
        out_shape=(shape(up_weight.shape),)
        + (shape((hidden, slab)),) * 2
        + (shape((slab, hidden)),),
        in_specs=[space, hbm, hbm],
        out_specs=(space,) * 4,
        scratch_shapes=[pltpu.VMEM(down_weight.shape, BF16), pltpu.SemaphoreType.DMA((2,))],
        compiler_params=params,
    )(gate_weight, in_hbm(up_weight), in_hbm(down_weight))

    chunks = [range(window // 2), range(window // 2, window)]
    counts = tuple(len(chunk) for chunk in chunks)
    own = [[arrived[d] for d in chunk] for chunk in chunks]
    other = [other_half(jnp.concatenate(v, axis=0)) for v in own]
    sums = []
    for i, count in enumerate(counts):
        n = count * PAIR
        take = (*own[i], other[i])
        if i == 0:
            part = call(
                functools.partial(product_kernel, count),
                shape((3 * n, hidden)),
                *take, gate_weight, up_w, down_t,
            )
            sums.append(reduced(part))
            continue
        part = call(
            functools.partial(gate_up_kernel, count),
            shape((2 * n, hidden)),
            *take, gate_weight, up_w,
        )
        h_part = call(functools.partial(hidden_kernel, count), shape((n, hidden)), *take, down_t)
        sums.append(reduced(part) + reduced(h_part))
    deltas, home = [], [None] * window
    for i, count in enumerate(counts):
        n = count * PAIR
        chunk = list(chunks[i])
        pieces = [chunk] if i == 0 else [chunk[count // 2 :], chunk[: count // 2]]
        sizes = [((piece[0] - chunk[0]) * PAIR, len(piece) * PAIR) for piece in pieces]
        *delta, = call(
            functools.partial(delta_kernel, len(sums[i]) // 2, sizes),
            (shape((2 * n, hidden)),) * 3
            + tuple(shape((size, w)) for _, size in sizes for _ in range(2)),
            *sums[i], gate_t, up_t,
        )
        deltas.append(delta[:3])
        for j, piece in enumerate(pieces):
            back_own, back_other = delta[3 + 2 * j], delta[4 + 2 * j]
            returned = other_half(back_other)
            back = (back_own.astype(F32) + returned.astype(F32)).astype(BF16)
            for k, d in enumerate(piece):
                block = back[k * PAIR : (k + 1) * PAIR]
                home[d] = across(block, d) if d else block

    blocks = tuple(v for i in range(len(chunks)) for v in (*own[i], other[i]))
    grad_args = blocks + tuple(delta[i] for i in (1, 2) for delta in deltas)
    gate_grad, up_grad = pl.pallas_call(
        functools.partial(gate_up_grad_kernel, counts),
        out_shape=(shape(gate_weight.shape),) * 2,
        in_specs=[space] * len(grad_args),
        out_specs=(hbm,) * 2,
        scratch_shapes=[pltpu.VMEM((4, w, hidden), BF16), pltpu.SemaphoreType.DMA((4,))],
        compiler_params=params,
    )(*grad_args)
    down_args = blocks + tuple(delta[0] for delta in deltas)
    out_shape = (shape(down_weight.shape),) if aligned else (shape((1, hidden, w)),) * 2
    down_grad = pl.pallas_call(
        functools.partial(down_grad_kernel, counts),
        out_shape=out_shape,
        in_specs=[space] * len(down_args),
        out_specs=(hbm,) * len(out_shape),
        scratch_shapes=[pltpu.VMEM((2, hidden, w), BF16), pltpu.SemaphoreType.DMA((2,))],
        compiler_params=params,
    )(*down_args)
    down_grad = down_grad[0] if aligned else jnp.concatenate(down_grad, axis=2)
    out_shape = (shape((tok, slab)),) if aligned else (shape((tok, w)),) * 2
    out = pl.pallas_call(
        functools.partial(combine_kernel, len(home)),
        out_shape=out_shape,
        in_specs=[space] * (len(home) + 2),
        out_specs=(hbm,) * len(out_shape),
        scratch_shapes=[pltpu.VMEM((2, tok, w), BF16), pltpu.SemaphoreType.DMA((4,))],
        compiler_params=params,
    )(*home, p0, p1)
    token_grad = out[0] if aligned else jnp.concatenate(out, axis=1)
    return token_grad, gate_grad, up_grad, down_grad


def solution(mesh):
    placed = (
        P("expert", "fsdp"),
        P("expert", "fsdp"),
        P("expert", None),
        P("expert", None),
        P("expert", "fsdp", None),
        P("expert", "fsdp", None),
        P("expert", None, "fsdp"),
    )
    return jax.shard_map(
        body,
        mesh=mesh,
        in_specs=placed,
        out_specs=(
            P("expert", "fsdp"),
            P("expert", "fsdp", None),
            P("expert", "fsdp", None),
            P("expert", None, "fsdp"),
        ),
        check_vma=False,
    )
```

```python
import functools

import jax
import jax.numpy as jnp
from jax import lax
from jax.experimental import pallas as pl
from jax.experimental.pallas import tpu as pltpu
from jax.sharding import PartitionSpec as P


CAP = 12
PAIR = 2 * CAP
BF16, F32 = jnp.bfloat16, jnp.float32
OVER_ROWS = (((0,), (0,)), ((), ()))


def dot(a, b, dims=None):
    if dims is None:
        dims = (((1,), (0,)), ((), ()))
    return lax.dot_general(a, b, dims, preferred_element_type=F32)


def upper(rows, columns):
    shape = (rows // PAIR, PAIR, columns)
    return (lax.broadcasted_iota(jnp.int32, shape, 1) < CAP).reshape(rows, columns)


def swapped(v, first):
    rows = v.shape[0]
    return jnp.where(first, pltpu.roll(v, rows - CAP, 0), pltpu.roll(v, CAP, 0))


def call(kernel, outs, *args, vmem=24, **kw):
    space = pl.BlockSpec(memory_space=pltpu.VMEM)
    return pl.pallas_call(
        kernel,
        out_shape=outs,
        in_specs=[space] * len(args),
        out_specs=jax.tree.map(lambda _: space, outs),
        compiler_params=pltpu.CompilerParams(vmem_limit_bytes=vmem << 20),
        **kw,
    )(*args)


def in_hbm(v):
    return pltpu.with_memory_space_constraint(v, pltpu.HBM)


def shape(dims, dtype=BF16):
    return jax.ShapeDtypeStruct(dims, dtype)


def columns(refs):
    if len(refs) == 2:
        return refs
    w = refs[0].shape[1] // 2
    return refs[0].at[:, 0:w], refs[0].at[:, w : 2 * w]


def place_kernel(window, halves, *refs):
    e_ref, ids_hbm, w_hbm = refs[:3]
    sources = columns(refs[3 : 3 + halves]) + columns(refs[3 + halves : 3 + 2 * halves])
    outs = refs[3 + 2 * halves : -4]
    held, ids_ref, w_ref, sems = refs[-4:]
    messages, (p0_ref, p1_ref) = outs[:window], outs[window:]
    top, tok = ids_ref.shape
    copies = [pltpu.make_async_copy(src, dst, sem) for src, dst, sem in zip(
        (ids_hbm, w_hbm) + tuple(sources),
        (ids_ref, w_ref) + tuple(held.at[i // 2, tok * (i % 2) : tok * (i % 2 + 1)] for i in range(4)),
        [sems.at[i] for i in range(6)],
    )]
    for copy in copies:
        copy.start()
    top, tok = ids_ref.shape
    dims = (window, PAIR, tok)
    rows = window * PAIR
    expert = lax.broadcasted_iota(jnp.int32, dims, 0) ^ e_ref[0]
    slot = lax.broadcasted_iota(jnp.int32, dims, 1).astype(F32).reshape(rows, tok)
    before = lax.broadcasted_iota(jnp.int32, (tok, tok), 0) < lax.broadcasted_iota(
        jnp.int32, (tok, tok), 1
    )
    before = before.astype(F32).astype(BF16)
    hit = jnp.zeros(dims, F32)
    weight = jnp.zeros(dims, F32)
    copies[0].wait()
    copies[1].wait()
    for k in range(top):
        same = ids_ref[k : k + 1, :][None] == expert
        hit = jnp.where(same, 1.0, hit)
        weight = jnp.where(same, w_ref[k : k + 1, :][None], weight)
    hit = hit.reshape(rows, tok)
    weight = weight.reshape(rows, tok)
    rank = dot(hit.astype(BF16), before)
    p0 = jnp.where(rank == slot, hit, 0.0)
    p1 = jnp.where(rank + CAP == slot, hit, 0.0)
    scale = jnp.sum((p0 + p1) * weight, axis=1, keepdims=True)
    p0, p1 = p0.astype(BF16), p1.astype(BF16)
    p0_ref[...] = p0
    p1_ref[...] = p1
    both = jnp.concatenate([p0, p1], axis=1)
    copies[2].wait()
    copies[3].wait()
    message = dot(both, held[0])
    for d in range(window):
        messages[d][:PAIR] = message[d * PAIR : (d + 1) * PAIR].astype(BF16)
    copies[4].wait()
    copies[5].wait()
    message = dot(both, held[1]) * scale
    for d in range(window):
        messages[d][PAIR:] = message[d * PAIR : (d + 1) * PAIR].astype(BF16)


def load_kernel(*refs):
    sources, held = refs[:3], refs[3:5] + refs[8:9]
    turned, sems = refs[5:8], refs[9]
    copies = [pltpu.make_async_copy(sources[i], held[i], sems.at[i]) for i in range(3)]
    for copy in copies:
        copy.start()
    for copy, ref, out in zip(copies, held, turned):
        copy.wait()
        out[...] = ref[0].T


def joined(refs):
    return jnp.concatenate([r[...].astype(F32) for r in refs], axis=0)


def received(own, other, part):
    take = slice(part * PAIR, (part + 1) * PAIR)
    blocks = [ref[take].astype(F32) for ref in own]
    for d in range(len(own)):
        start = 2 * d * PAIR + part * PAIR
        blocks.append(other[start : start + PAIR].astype(F32))
    return jnp.concatenate(blocks, axis=0)


def unfolded(v):
    first = upper(*v.shape)
    turned = swapped(v, first)
    low, high = jnp.where(first, v, turned), jnp.where(first, turned, v)
    return jnp.concatenate([low.astype(BF16), high.astype(BF16)], axis=1)


def gate_up_kernel(count, *refs):
    own, other, (gate_ref, up_ref, out_ref) = refs[:count], refs[count], refs[count + 1 :]
    rows = unfolded(received(own, other, 0))
    gate, up = dot(rows, gate_ref[0]), dot(rows, up_ref[0])
    out_ref[: gate.shape[0]] = jnp.where(upper(*gate.shape), gate, up).astype(BF16)


def hidden_kernel(count, *refs):
    own, other, (down_ref, out_ref) = refs[:count], refs[count], refs[count + 1 :]
    n = count * PAIR
    grads = unfolded(received(own, other, 1))
    part = dot(grads, down_ref[...])
    start = out_ref.shape[0] - n
    out_ref[start:] = jnp.where(upper(n, part.shape[1]), part[:n], part[n:]).astype(BF16)


def product_kernel(count, *refs):
    blocks, (gate_ref, up_ref, down_ref, out_ref) = refs[: count + 1], refs[count + 1 :]
    gate_up_kernel(count, *blocks, gate_ref, up_ref, out_ref)
    hidden_kernel(count, *blocks, down_ref, out_ref)


def delta_kernel(pairs, sizes, *refs):
    sums, refs = refs[: 2 * pairs], refs[2 * pairs :]
    (gate_ref, up_ref, act_ref, gd_ref, ud_ref), backs = refs[:5], refs[5:]
    n, w = act_ref.shape[0] // 2, backs[0].shape[1]
    totals = [
        sums[2 * i][...].astype(F32) + sums[2 * i + 1][...].astype(F32) for i in range(pairs)
    ]
    gu, h = totals if pairs == 2 else (totals[0][: 2 * n], totals[0][2 * n :])
    first = upper(*gu.shape)
    half = upper(*h.shape)
    gu_t, h_t = swapped(gu, first), swapped(h, half)
    gate, up = jnp.where(first, gu, gu_t), jnp.where(first, gu_t, gu)
    hidden = jnp.concatenate([jnp.where(half, h, h_t), jnp.where(half, h_t, h)], axis=0)
    sig = jax.nn.sigmoid(gate)
    act_ref[...] = (gate * sig * up).astype(BF16)
    gate_delta = hidden * up * sig * (1.0 + gate * (1.0 - sig))
    up_delta = hidden * gate * sig
    gate_delta, up_delta = gate_delta.astype(BF16), up_delta.astype(BF16)
    gd_ref[...] = gate_delta
    ud_ref[...] = up_delta
    back = dot(gate_delta, gate_ref[...]) + dot(up_delta, up_ref[...])
    back = jnp.where(upper(2 * n, w), back[:, :w], back[:, w:]).astype(BF16)
    for i, (start, size) in enumerate(sizes):
        backs[2 * i][...] = back[start : start + size]
        backs[2 * i + 1][...] = back[n + start : n + start + size]


def all_received(counts, refs, part):
    blocks, at = [], 0
    for count in counts:
        blocks.append(received(refs[at : at + count], refs[at + count], part))
        at += count + 1
    return jnp.concatenate(blocks, axis=0), refs[at:]


def gate_up_grad_kernel(counts, *refs):
    rows, refs = all_received(counts, refs, 0)
    k = len(counts)
    deltas = [jnp.concatenate([r[...].astype(F32) for r in refs[i * k : i * k + k]], axis=0) for i in (0, 1)]
    outs, (held, sems) = refs[2 * k : -2], refs[-2:]
    w = rows.shape[1]
    first = upper(*deltas[0].shape)
    turned = rows.T.astype(BF16)
    copies = []
    for half in (0, 1):
        keep = first if half == 0 else jnp.logical_not(first)
        for i, delta in enumerate(deltas):
            at = 2 * half + i
            held[at] = dot(turned, jnp.where(keep, delta, 0.0).astype(BF16)).astype(BF16)
            copies.append(
                pltpu.make_async_copy(
                    held.at[at], outs[i].at[0, half * w : (half + 1) * w], sems.at[at]
                )
            )
            copies[-1].start()
    for copy in copies:
        copy.wait()


def down_grad_kernel(counts, *refs):
    grads, refs = all_received(counts, refs, 1)
    k = len(counts)
    act = jnp.concatenate([r[...].astype(F32) for r in refs[:k]], axis=0)
    outs, (held, sems) = refs[k:-2], refs[-2:]
    w = grads.shape[1]
    grads = grads.astype(BF16)
    first = upper(*act.shape)
    copies = []
    for half in (0, 1):
        keep = first if half == 0 else jnp.logical_not(first)
        held[half] = dot(jnp.where(keep, act, 0.0).astype(BF16), grads, OVER_ROWS).astype(BF16)
        out = outs[0].at[0, :, half * w : (half + 1) * w] if len(outs) == 1 else outs[half].at[0]
        copies.append(pltpu.make_async_copy(held.at[half], out, sems.at[half]))
        copies[-1].start()
    for copy in copies:
        copy.wait()


def combine_kernel(count, *refs):
    blocks, (p0_ref, p1_ref) = refs[:count], refs[count : count + 2]
    outs, (held, sems) = refs[count + 2 : -2], refs[-2:]
    rows = joined(blocks).astype(BF16)
    copies = []
    tok = p0_ref.shape[1]
    for k in range(4):
        here = slice(k * tok // 4, (k + 1) * tok // 4)
        for i, (p_ref, out) in enumerate(zip((p0_ref, p1_ref), columns(outs))):
            held[i, here] = dot(p_ref[:, here], rows, OVER_ROWS).astype(BF16)
            copies.append(
                pltpu.make_async_copy(held.at[i, here], out.at[here], sems.at[2 * k + i])
            )
            copies[-1].start()
    for copy in copies:
        copy.wait()


def body(tokens, output_grad, route_weight, expert_ids, gate_weight, up_weight, down_weight):
    expert_count, fsdp_count = lax.axis_size("expert"), lax.axis_size("fsdp")
    window = expert_count // 2
    tok, slab = tokens.shape
    w = slab // 2
    aligned = w % 128 == 0
    hidden = gate_weight.shape[2]
    rows = window * PAIR
    first_expert = lax.shift_right_logical(lax.axis_index("expert"), 1).reshape(1)

    def across(v, d):
        perm = [(c * 2 + h, (c ^ d) * 2 + h) for c in range(window) for h in range(2)]
        return lax.ppermute(v, "expert", perm)

    def other_half(v):
        return lax.ppermute(v, "expert", [(e, e ^ 1) for e in range(expert_count)])

    def reduced(part):
        bit = 1
        while bit < fsdp_count:
            last = bit * 2 >= fsdp_count
            got = lax.ppermute(part, "fsdp", [(f, f ^ bit) for f in range(fsdp_count)])
            if last:
                return part, got
            part = (part.astype(F32) + got.astype(F32)).astype(BF16)
            bit *= 2

    def halves(v):
        return (v,) if aligned else (v[:, :w], v[:, w:])

    space = pl.BlockSpec(memory_space=pltpu.VMEM)
    smem = pl.BlockSpec(memory_space=pltpu.SMEM)
    hbm = pl.BlockSpec(memory_space=pltpu.HBM)
    params = pltpu.CompilerParams(vmem_limit_bytes=16 << 20)
    message = shape((2 * PAIR, w))
    far = halves(tokens) + halves(output_grad)
    placed = pl.pallas_call(
        functools.partial(place_kernel, window, len(far) // 2),
        out_shape=(message,) * window + (shape((rows, tok)),) * 2,
        in_specs=[smem] + [hbm] * (2 + len(far)),
        out_specs=(space,) * (window + 2),
        scratch_shapes=[
            pltpu.VMEM((2, 2 * tok, w), BF16),
            pltpu.VMEM(expert_ids.shape[::-1], jnp.int32),
            pltpu.VMEM(route_weight.shape[::-1], F32),
            pltpu.SemaphoreType.DMA((6,)),
        ],
        compiler_params=params,
    )(first_expert, *(in_hbm(v) for v in (expert_ids.T, route_weight.T, *far)))
    p0, p1 = placed[window:]
    arrived = [placed[0]] + [across(placed[k], k) for k in range(1, window)]
    gate_w, up_w, gate_t, up_t, down_t = pl.pallas_call(
        load_kernel,
        out_shape=(shape(gate_weight.shape),) * 2
        + (shape((hidden, slab)),) * 2
        + (shape((slab, hidden)),),
        in_specs=[hbm] * 3,
        out_specs=(space,) * 5,
        scratch_shapes=[pltpu.VMEM(down_weight.shape, BF16), pltpu.SemaphoreType.DMA((3,))],
        compiler_params=params,
    )(in_hbm(gate_weight), in_hbm(up_weight), in_hbm(down_weight))

    chunks = [range(window // 2), range(window // 2, window)]
    counts = tuple(len(chunk) for chunk in chunks)
    own = [[arrived[d] for d in chunk] for chunk in chunks]
    other = [other_half(jnp.concatenate(v, axis=0)) for v in own]
    sums = []
    for i, count in enumerate(counts):
        n = count * PAIR
        take = (*own[i], other[i])
        if i == 0:
            part = call(
                functools.partial(product_kernel, count),
                shape((3 * n, hidden)),
                *take, gate_w, up_w, down_t,
            )
            sums.append(reduced(part))
            continue
        part = call(
            functools.partial(gate_up_kernel, count),
            shape((2 * n, hidden)),
            *take, gate_w, up_w,
        )
        h_part = call(functools.partial(hidden_kernel, count), shape((n, hidden)), *take, down_t)
        sums.append(reduced(part) + reduced(h_part))
    deltas, home = [], [None] * window
    for i, count in enumerate(counts):
        n = count * PAIR
        chunk = list(chunks[i])
        pieces = [chunk] if i == 0 else [chunk[count // 2 :], chunk[: count // 2]]
        sizes = [((piece[0] - chunk[0]) * PAIR, len(piece) * PAIR) for piece in pieces]
        *delta, = call(
            functools.partial(delta_kernel, len(sums[i]) // 2, sizes),
            (shape((2 * n, hidden)),) * 3
            + tuple(shape((size, w)) for _, size in sizes for _ in range(2)),
            *sums[i], gate_t, up_t,
        )
        deltas.append(delta[:3])
        for j, piece in enumerate(pieces):
            back_own, back_other = delta[3 + 2 * j], delta[4 + 2 * j]
            returned = other_half(back_other)
            back = (back_own.astype(F32) + returned.astype(F32)).astype(BF16)
            for k, d in enumerate(piece):
                block = back[k * PAIR : (k + 1) * PAIR]
                home[d] = across(block, d) if d else block

    blocks = tuple(v for i in range(len(chunks)) for v in (*own[i], other[i]))
    grad_args = blocks + tuple(delta[i] for i in (1, 2) for delta in deltas)
    gate_grad, up_grad = pl.pallas_call(
        functools.partial(gate_up_grad_kernel, counts),
        out_shape=(shape(gate_weight.shape),) * 2,
        in_specs=[space] * len(grad_args),
        out_specs=(hbm,) * 2,
        scratch_shapes=[pltpu.VMEM((4, w, hidden), BF16), pltpu.SemaphoreType.DMA((4,))],
        compiler_params=params,
    )(*grad_args)
    down_args = blocks + tuple(delta[0] for delta in deltas)
    out_shape = (shape(down_weight.shape),) if aligned else (shape((1, hidden, w)),) * 2
    down_grad = pl.pallas_call(
        functools.partial(down_grad_kernel, counts),
        out_shape=out_shape,
        in_specs=[space] * len(down_args),
        out_specs=(hbm,) * len(out_shape),
        scratch_shapes=[pltpu.VMEM((2, hidden, w), BF16), pltpu.SemaphoreType.DMA((2,))],
        compiler_params=params,
    )(*down_args)
    down_grad = down_grad[0] if aligned else jnp.concatenate(down_grad, axis=2)
    out_shape = (shape((tok, slab)),) if aligned else (shape((tok, w)),) * 2
    out = pl.pallas_call(
        functools.partial(combine_kernel, len(home)),
        out_shape=out_shape,
        in_specs=[space] * (len(home) + 2),
        out_specs=(hbm,) * len(out_shape),
        scratch_shapes=[pltpu.VMEM((2, tok, w), BF16), pltpu.SemaphoreType.DMA((8,))],
        compiler_params=params,
    )(*home, p0, p1)
    token_grad = out[0] if aligned else jnp.concatenate(out, axis=1)
    return token_grad, gate_grad, up_grad, down_grad


def solution(mesh):
    placed = (
        P("expert", "fsdp"),
        P("expert", "fsdp"),
        P("expert", None),
        P("expert", None),
        P("expert", "fsdp", None),
        P("expert", "fsdp", None),
        P("expert", None, "fsdp"),
    )
    return jax.shard_map(
        body,
        mesh=mesh,
        in_specs=placed,
        out_specs=(
            P("expert", "fsdp"),
            P("expert", "fsdp", None),
            P("expert", "fsdp", None),
            P("expert", None, "fsdp"),
        ),
        check_vma=False,
    )
```

```python
import functools

import jax
import jax.numpy as jnp
from jax import lax
from jax.experimental import pallas as pl
from jax.experimental.pallas import tpu as pltpu
from jax.sharding import PartitionSpec as P


CAP = 12
PAIR = 2 * CAP
BF16, F32 = jnp.bfloat16, jnp.float32
OVER_ROWS = (((0,), (0,)), ((), ()))


def dot(a, b, dims=None):
    if dims is None:
        dims = (((1,), (0,)), ((), ()))
    return lax.dot_general(a, b, dims, preferred_element_type=F32)


def upper(rows, columns):
    shape = (rows // PAIR, PAIR, columns)
    return (lax.broadcasted_iota(jnp.int32, shape, 1) < CAP).reshape(rows, columns)


def swapped(v, first):
    rows = v.shape[0]
    return jnp.where(first, pltpu.roll(v, rows - CAP, 0), pltpu.roll(v, CAP, 0))


def call(kernel, outs, *args, vmem=24, **kw):
    space = pl.BlockSpec(memory_space=pltpu.VMEM)
    return pl.pallas_call(
        kernel,
        out_shape=outs,
        in_specs=[space] * len(args),
        out_specs=jax.tree.map(lambda _: space, outs),
        compiler_params=pltpu.CompilerParams(vmem_limit_bytes=vmem << 20),
        **kw,
    )(*args)


def in_hbm(v):
    return pltpu.with_memory_space_constraint(v, pltpu.HBM)


def shape(dims, dtype=BF16):
    return jax.ShapeDtypeStruct(dims, dtype)


def columns(refs):
    if len(refs) == 2:
        return refs
    w = refs[0].shape[1] // 2
    return refs[0].at[:, 0:w], refs[0].at[:, w : 2 * w]


def place_kernel(window, halves, *refs):
    e_ref, ids_hbm, w_hbm = refs[:3]
    sources = columns(refs[3 : 3 + halves]) + columns(refs[3 + halves : 3 + 2 * halves])
    outs = refs[3 + 2 * halves : -4]
    held, ids_ref, w_ref, sems = refs[-4:]
    messages, (p0_ref, p1_ref) = outs[:window], outs[window:]
    top, tok = ids_ref.shape
    copies = [pltpu.make_async_copy(src, dst, sem) for src, dst, sem in zip(
        (ids_hbm, w_hbm) + tuple(sources),
        (ids_ref, w_ref) + tuple(held.at[i // 2, tok * (i % 2) : tok * (i % 2 + 1)] for i in range(4)),
        [sems.at[i] for i in range(6)],
    )]
    for copy in copies:
        copy.start()
    top, tok = ids_ref.shape
    dims = (window, PAIR, tok)
    rows = window * PAIR
    expert = lax.broadcasted_iota(jnp.int32, dims, 0) ^ e_ref[0]
    slot = lax.broadcasted_iota(jnp.int32, dims, 1).astype(F32).reshape(rows, tok)
    before = lax.broadcasted_iota(jnp.int32, (tok, tok), 0) < lax.broadcasted_iota(
        jnp.int32, (tok, tok), 1
    )
    before = before.astype(F32).astype(BF16)
    hit = jnp.zeros(dims, F32)
    weight = jnp.zeros(dims, F32)
    copies[0].wait()
    copies[1].wait()
    for k in range(top):
        same = ids_ref[k : k + 1, :][None] == expert
        hit = jnp.where(same, 1.0, hit)
        weight = jnp.where(same, w_ref[k : k + 1, :][None], weight)
    hit = hit.reshape(rows, tok)
    weight = weight.reshape(rows, tok)
    rank = dot(hit.astype(BF16), before)
    p0 = jnp.where(rank == slot, hit, 0.0)
    p1 = jnp.where(rank + CAP == slot, hit, 0.0)
    scale = jnp.sum((p0 + p1) * weight, axis=1, keepdims=True)
    p0, p1 = p0.astype(BF16), p1.astype(BF16)
    p0_ref[...] = p0
    p1_ref[...] = p1
    copies[2].wait()
    message = dot(p0, held[0, :tok])
    copies[3].wait()
    message = message + dot(p1, held[0, tok:])
    for d in range(window):
        messages[d][:PAIR] = message[d * PAIR : (d + 1) * PAIR].astype(BF16)
    copies[4].wait()
    message = dot(p0, held[1, :tok])
    copies[5].wait()
    message = (message + dot(p1, held[1, tok:])) * scale
    for d in range(window):
        messages[d][PAIR:] = message[d * PAIR : (d + 1) * PAIR].astype(BF16)


def load_kernel(*refs):
    sources, held = refs[:3], refs[3:5] + refs[8:9]
    turned, sems = refs[5:8], refs[9]
    copies = [pltpu.make_async_copy(sources[i], held[i], sems.at[i]) for i in range(3)]
    for copy in copies:
        copy.start()
    for copy, ref, out in zip(copies, held, turned):
        copy.wait()
        out[...] = ref[0].T


def joined(refs):
    return jnp.concatenate([r[...].astype(F32) for r in refs], axis=0)


def received(own, other, part):
    take = slice(part * PAIR, (part + 1) * PAIR)
    blocks = [ref[take].astype(F32) for ref in own]
    for d in range(len(own)):
        start = 2 * d * PAIR + part * PAIR
        blocks.append(other[start : start + PAIR].astype(F32))
    return jnp.concatenate(blocks, axis=0)


def unfolded(v):
    first = upper(*v.shape)
    turned = swapped(v, first)
    low, high = jnp.where(first, v, turned), jnp.where(first, turned, v)
    return jnp.concatenate([low.astype(BF16), high.astype(BF16)], axis=1)


def gate_up_kernel(count, *refs):
    own, other, (gate_ref, up_ref, out_ref) = refs[:count], refs[count], refs[count + 1 :]
    rows = unfolded(received(own, other, 0))
    gate, up = dot(rows, gate_ref[0]), dot(rows, up_ref[0])
    out_ref[: gate.shape[0]] = jnp.where(upper(*gate.shape), gate, up).astype(BF16)


def hidden_kernel(count, *refs):
    own, other, (down_ref, out_ref) = refs[:count], refs[count], refs[count + 1 :]
    n = count * PAIR
    grads = unfolded(received(own, other, 1))
    part = dot(grads, down_ref[...])
    start = out_ref.shape[0] - n
    out_ref[start:] = jnp.where(upper(n, part.shape[1]), part[:n], part[n:]).astype(BF16)


def product_kernel(count, *refs):
    blocks, (gate_ref, up_ref, down_ref, out_ref) = refs[: count + 1], refs[count + 1 :]
    gate_up_kernel(count, *blocks, gate_ref, up_ref, out_ref)
    hidden_kernel(count, *blocks, down_ref, out_ref)


def delta_kernel(pairs, sizes, *refs):
    sums, refs = refs[: 2 * pairs], refs[2 * pairs :]
    (gate_ref, up_ref, act_ref, gd_ref, ud_ref), backs = refs[:5], refs[5:]
    n, w = act_ref.shape[0] // 2, backs[0].shape[1]
    totals = [
        sums[2 * i][...].astype(F32) + sums[2 * i + 1][...].astype(F32) for i in range(pairs)
    ]
    gu, h = totals if pairs == 2 else (totals[0][: 2 * n], totals[0][2 * n :])
    first = upper(*gu.shape)
    half = upper(*h.shape)
    gu_t, h_t = swapped(gu, first), swapped(h, half)
    gate, up = jnp.where(first, gu, gu_t), jnp.where(first, gu_t, gu)
    hidden = jnp.concatenate([jnp.where(half, h, h_t), jnp.where(half, h_t, h)], axis=0)
    sig = jax.nn.sigmoid(gate)
    act_ref[...] = (gate * sig * up).astype(BF16)
    gate_delta = hidden * up * sig * (1.0 + gate * (1.0 - sig))
    up_delta = hidden * gate * sig
    gate_delta, up_delta = gate_delta.astype(BF16), up_delta.astype(BF16)
    gd_ref[...] = gate_delta
    ud_ref[...] = up_delta
    back = dot(gate_delta, gate_ref[...]) + dot(up_delta, up_ref[...])
    back = jnp.where(upper(2 * n, w), back[:, :w], back[:, w:]).astype(BF16)
    for i, (start, size) in enumerate(sizes):
        backs[2 * i][...] = back[start : start + size]
        backs[2 * i + 1][...] = back[n + start : n + start + size]


def all_received(counts, refs, part):
    blocks, at = [], 0
    for count in counts:
        blocks.append(received(refs[at : at + count], refs[at + count], part))
        at += count + 1
    return jnp.concatenate(blocks, axis=0), refs[at:]


def gate_up_grad_kernel(counts, *refs):
    rows, refs = all_received(counts, refs, 0)
    k = len(counts)
    deltas = [jnp.concatenate([r[...].astype(F32) for r in refs[i * k : i * k + k]], axis=0) for i in (0, 1)]
    outs, (held, sems) = refs[2 * k : -2], refs[-2:]
    w = rows.shape[1]
    first = upper(*deltas[0].shape)
    turned = rows.T.astype(BF16)
    copies = []
    for half in (0, 1):
        keep = first if half == 0 else jnp.logical_not(first)
        for i, delta in enumerate(deltas):
            at = 2 * half + i
            held[at] = dot(turned, jnp.where(keep, delta, 0.0).astype(BF16)).astype(BF16)
            copies.append(
                pltpu.make_async_copy(
                    held.at[at], outs[i].at[0, half * w : (half + 1) * w], sems.at[at]
                )
            )
            copies[-1].start()
    for copy in copies:
        copy.wait()


def down_grad_kernel(counts, *refs):
    grads, refs = all_received(counts, refs, 1)
    k = len(counts)
    act = jnp.concatenate([r[...].astype(F32) for r in refs[:k]], axis=0)
    outs, (held, sems) = refs[k:-2], refs[-2:]
    w = grads.shape[1]
    grads = grads.astype(BF16)
    first = upper(*act.shape)
    copies = []
    for half in (0, 1):
        keep = first if half == 0 else jnp.logical_not(first)
        held[half] = dot(jnp.where(keep, act, 0.0).astype(BF16), grads, OVER_ROWS).astype(BF16)
        out = outs[0].at[0, :, half * w : (half + 1) * w] if len(outs) == 1 else outs[half].at[0]
        copies.append(pltpu.make_async_copy(held.at[half], out, sems.at[half]))
        copies[-1].start()
    for copy in copies:
        copy.wait()


def combine_kernel(count, *refs):
    blocks, (p0_ref, p1_ref) = refs[:count], refs[count : count + 2]
    outs, (held, sems) = refs[count + 2 : -2], refs[-2:]
    rows = joined(blocks).astype(BF16)
    copies = []
    tok = p0_ref.shape[1]
    for k in range(4):
        here = slice(k * tok // 4, (k + 1) * tok // 4)
        for i, (p_ref, out) in enumerate(zip((p0_ref, p1_ref), columns(outs))):
            held[i, here] = dot(p_ref[:, here], rows, OVER_ROWS).astype(BF16)
            copies.append(
                pltpu.make_async_copy(held.at[i, here], out.at[here], sems.at[2 * k + i])
            )
            copies[-1].start()
    for copy in copies:
        copy.wait()


def body(tokens, output_grad, route_weight, expert_ids, gate_weight, up_weight, down_weight):
    expert_count, fsdp_count = lax.axis_size("expert"), lax.axis_size("fsdp")
    window = expert_count // 2
    tok, slab = tokens.shape
    w = slab // 2
    aligned = w % 128 == 0
    hidden = gate_weight.shape[2]
    rows = window * PAIR
    first_expert = lax.shift_right_logical(lax.axis_index("expert"), 1).reshape(1)

    def across(v, d):
        perm = [(c * 2 + h, (c ^ d) * 2 + h) for c in range(window) for h in range(2)]
        return lax.ppermute(v, "expert", perm)

    def other_half(v):
        return lax.ppermute(v, "expert", [(e, e ^ 1) for e in range(expert_count)])

    def reduced(part):
        bit = 1
        while bit < fsdp_count:
            last = bit * 2 >= fsdp_count
            got = lax.ppermute(part, "fsdp", [(f, f ^ bit) for f in range(fsdp_count)])
            if last:
                return part, got
            part = (part.astype(F32) + got.astype(F32)).astype(BF16)
            bit *= 2

    def halves(v):
        return (v,) if aligned else (v[:, :w], v[:, w:])

    space = pl.BlockSpec(memory_space=pltpu.VMEM)
    smem = pl.BlockSpec(memory_space=pltpu.SMEM)
    hbm = pl.BlockSpec(memory_space=pltpu.HBM)
    params = pltpu.CompilerParams(vmem_limit_bytes=16 << 20)
    message = shape((2 * PAIR, w))
    far = halves(tokens) + halves(output_grad)
    placed = pl.pallas_call(
        functools.partial(place_kernel, window, len(far) // 2),
        out_shape=(message,) * window + (shape((rows, tok)),) * 2,
        in_specs=[smem] + [hbm] * (2 + len(far)),
        out_specs=(space,) * (window + 2),
        scratch_shapes=[
            pltpu.VMEM((2, 2 * tok, w), BF16),
            pltpu.VMEM(expert_ids.shape[::-1], jnp.int32),
            pltpu.VMEM(route_weight.shape[::-1], F32),
            pltpu.SemaphoreType.DMA((6,)),
        ],
        compiler_params=params,
    )(first_expert, *(in_hbm(v) for v in (expert_ids.T, route_weight.T, *far)))
    p0, p1 = placed[window:]
    arrived = [placed[0]] + [across(placed[k], k) for k in range(1, window)]
    gate_w, up_w, gate_t, up_t, down_t = pl.pallas_call(
        load_kernel,
        out_shape=(shape(gate_weight.shape),) * 2
        + (shape((hidden, slab)),) * 2
        + (shape((slab, hidden)),),
        in_specs=[hbm] * 3,
        out_specs=(space,) * 5,
        scratch_shapes=[pltpu.VMEM(down_weight.shape, BF16), pltpu.SemaphoreType.DMA((3,))],
        compiler_params=params,
    )(in_hbm(gate_weight), in_hbm(up_weight), in_hbm(down_weight))

    chunks = [range(window // 2), range(window // 2, window)]
    counts = tuple(len(chunk) for chunk in chunks)
    own = [[arrived[d] for d in chunk] for chunk in chunks]
    other = [other_half(jnp.concatenate(v, axis=0)) for v in own]
    sums = []
    for i, count in enumerate(counts):
        n = count * PAIR
        take = (*own[i], other[i])
        if i == 0:
            part = call(
                functools.partial(product_kernel, count),
                shape((3 * n, hidden)),
                *take, gate_w, up_w, down_t,
            )
            sums.append(reduced(part))
            continue
        part = call(
            functools.partial(gate_up_kernel, count),
            shape((2 * n, hidden)),
            *take, gate_w, up_w,
        )
        h_part = call(functools.partial(hidden_kernel, count), shape((n, hidden)), *take, down_t)
        sums.append(reduced(part) + reduced(h_part))
    deltas, home = [], [None] * window
    for i, count in enumerate(counts):
        n = count * PAIR
        chunk = list(chunks[i])
        pieces = [chunk] if i == 0 else [chunk[count // 2 :], chunk[: count // 2]]
        sizes = [((piece[0] - chunk[0]) * PAIR, len(piece) * PAIR) for piece in pieces]
        *delta, = call(
            functools.partial(delta_kernel, len(sums[i]) // 2, sizes),
            (shape((2 * n, hidden)),) * 3
            + tuple(shape((size, w)) for _, size in sizes for _ in range(2)),
            *sums[i], gate_t, up_t,
        )
        deltas.append(delta[:3])
        for j, piece in enumerate(pieces):
            back_own, back_other = delta[3 + 2 * j], delta[4 + 2 * j]
            returned = other_half(back_other)
            back = (back_own.astype(F32) + returned.astype(F32)).astype(BF16)
            for k, d in enumerate(piece):
                block = back[k * PAIR : (k + 1) * PAIR]
                home[d] = across(block, d) if d else block

    blocks = tuple(v for i in range(len(chunks)) for v in (*own[i], other[i]))
    grad_args = blocks + tuple(delta[i] for i in (1, 2) for delta in deltas)
    gate_grad, up_grad = pl.pallas_call(
        functools.partial(gate_up_grad_kernel, counts),
        out_shape=(shape(gate_weight.shape),) * 2,
        in_specs=[space] * len(grad_args),
        out_specs=(hbm,) * 2,
        scratch_shapes=[pltpu.VMEM((4, w, hidden), BF16), pltpu.SemaphoreType.DMA((4,))],
        compiler_params=params,
    )(*grad_args)
    down_args = blocks + tuple(delta[0] for delta in deltas)
    out_shape = (shape(down_weight.shape),) if aligned else (shape((1, hidden, w)),) * 2
    down_grad = pl.pallas_call(
        functools.partial(down_grad_kernel, counts),
        out_shape=out_shape,
        in_specs=[space] * len(down_args),
        out_specs=(hbm,) * len(out_shape),
        scratch_shapes=[pltpu.VMEM((2, hidden, w), BF16), pltpu.SemaphoreType.DMA((2,))],
        compiler_params=params,
    )(*down_args)
    down_grad = down_grad[0] if aligned else jnp.concatenate(down_grad, axis=2)
    out_shape = (shape((tok, slab)),) if aligned else (shape((tok, w)),) * 2
    out = pl.pallas_call(
        functools.partial(combine_kernel, len(home)),
        out_shape=out_shape,
        in_specs=[space] * (len(home) + 2),
        out_specs=(hbm,) * len(out_shape),
        scratch_shapes=[pltpu.VMEM((2, tok, w), BF16), pltpu.SemaphoreType.DMA((8,))],
        compiler_params=params,
    )(*home, p0, p1)
    token_grad = out[0] if aligned else jnp.concatenate(out, axis=1)
    return token_grad, gate_grad, up_grad, down_grad


def solution(mesh):
    placed = (
        P("expert", "fsdp"),
        P("expert", "fsdp"),
        P("expert", None),
        P("expert", None),
        P("expert", "fsdp", None),
        P("expert", "fsdp", None),
        P("expert", None, "fsdp"),
    )
    return jax.shard_map(
        body,
        mesh=mesh,
        in_specs=placed,
        out_specs=(
            P("expert", "fsdp"),
            P("expert", "fsdp", None),
            P("expert", "fsdp", None),
            P("expert", None, "fsdp"),
        ),
        check_vma=False,
    )
```
